512 devices in a mesh: chan: 128 (over z, y, core), win: 4 (over x).
Axes of the slice: x: 4, y: 8, z: 8, core: 2. Of those that a mesh axis runs over, the one named last changes fastest.
Arguments:
- receivers: bfloat16 [8, 1024, 512], P('win', 'chan'), may hold values from -6 to 6
- sources: bfloat16 [8, 32768, 512], P('win', 'chan'), may hold values from -6 to 6
- coupling: float32 [1024], P('chan')
- lag_basis: float32 [200, 32], replicated, may hold values from -0.4375 to 0.4375
- source_order: int32 [2], replicated, may hold values from 0 to 127
Outputs:
- gather_projections: float32 [2, 1024, 32, 256], P(None, 'chan', None, 'win')
The draws below stay inside these ranges and needn't reach their ends.
Inputs may be any that keep to these rules, and one draw needn't show every extreme that they name: `source_order`: steps may name the same owner more than once.
All inputs are finite; a program needn't handle non-finite values.
Results may differ from the reference program's by a relative error of at most 0.0028.
Values may be sent and summed in bfloat16 or wider, within the bound.
A program may use at most 64 MiB of HBM per device.

```python
import math
import jax
import jax.numpy as jnp
from jax import lax

FREQS = 256
LAGS = 200
SRC = 256
K = 32
STEPS = 2
CHANNELS = 1024
OWNERS = 128
WINDOWS = 8


def draw_coupling(key, part):
    position = jnp.arange(CHANNELS, dtype=jnp.float32) / max(CHANNELS - 1, 1)
    trend = jnp.exp(jnp.log(3.0) * position)
    jitter = jnp.exp(jax.random.uniform(key, (CHANNELS,), jnp.float32, 0.0, jnp.log(3.0)))
    return trend * jitter


def level_of(stream_key, shape, shards, least, high):
    def one(dim, parts):
        steps = jax.random.uniform(jax.random.fold_in(jax.random.fold_in(stream_key, 6), dim), (parts,), jnp.float32, least / len(shards), high / len(shards))
        return jnp.repeat(jnp.exp(steps), shape[dim] // parts).reshape((-1,) + (1,) * (len(shape) - dim - 1))

    gain = one(*shards[0])
    for cut in shards[1:]:
        gain = gain * one(*cut)
    return gain


def scatter_about(own_key, shape, scale, most, split=(), kind=jnp.bfloat16):
    result = scale * jax.random.normal(own_key, shape, jnp.float32)
    if split:
        result = result * level_of(own_key, shape, split, -0.22, 0.18)
    return jnp.clip(result, -most, most).astype(kind)


def setup_inputs(seed: int = 0) -> dict:
    splits = jax.random.split(jax.random.key(seed), 6)
    receivers = scatter_about(splits[0], (WINDOWS, CHANNELS, 2 * FREQS), 1.0, 6.0, ((0, 4), (1, 128)))
    sources = scatter_about(splits[1], (WINDOWS, OWNERS * SRC, 2 * FREQS), 1.0, 6.0, ((0, 4), (1, 128)))
    coupling = draw_coupling(jax.random.fold_in(splits[5], 71), 0)
    lag_basis = scatter_about(splits[3], (LAGS, K), LAGS ** -0.5, 0.4375, (), jnp.float32)
    source_order = jax.random.randint(splits[4], (STEPS,), 0, OWNERS).astype(jnp.int32)
    return {"receivers": receivers, "sources": sources, "coupling": coupling, "lag_basis": lag_basis, "source_order": source_order}


def phase_tables(band_size, lag_count):
    frequency = jnp.arange(band_size, dtype=jnp.int32)
    lag_shift = jnp.arange(lag_count, dtype=jnp.int32) - lag_count // 2
    phase_turns = frequency[:, None] * lag_shift[None, :] % (2 * band_size)
    phase = phase_turns.astype(jnp.float32) * (math.pi / band_size)
    return (jnp.cos(phase).T, jnp.sin(phase).T)

def twist(spectra, cosine_table, sine_table):
    band_size = spectra.shape[-1] // 2
    real_part = spectra[..., None, :band_size].astype(jnp.float32)
    imag_part = spectra[..., None, band_size:].astype(jnp.float32)
    twisted_real = real_part * cosine_table - imag_part * sine_table
    twisted_imag = real_part * sine_table + imag_part * cosine_table
    return jnp.concatenate([twisted_real, twisted_imag], axis=-1).astype(jnp.bfloat16)

def reference(receivers, sources, coupling, lag_basis, source_order):
    cosine_table, sine_table = phase_tables(FREQS, LAGS)

    def add_window(stacked_sum, window_data):
        receiver_rows, source_rows = window_data
        twisted = lax.optimization_barrier(twist(receiver_rows, cosine_table, sine_table))
        twisted = twisted.astype(jnp.float32).reshape(CHANNELS * LAGS, 2 * FREQS)
        terms = []
        for step_index in range(STEPS):
            start = (source_order[step_index] * SRC).astype(jnp.int32)
            source_block = lax.dynamic_slice_in_dim(source_rows, start, SRC, 0).astype(jnp.float32)
            terms.append(jnp.dot(twisted, source_block.T))
        return (stacked_sum + jnp.stack(terms), None)
    initial = jnp.zeros((STEPS, CHANNELS * LAGS, SRC), jnp.float32)
    stacked_sum, unused = lax.scan(add_window, initial, (receivers, sources))
    gathers = stacked_sum.reshape(STEPS, CHANNELS, LAGS, SRC) * coupling[None, :, None, None]
    projections = jnp.einsum('bcls,lk->bcks', gathers, lag_basis, precision=lax.Precision.HIGHEST)
    power = lax.optimization_barrier(jnp.sum(projections * projections, axis=(1, 2))) / (CHANNELS * K)
    return projections * lax.rsqrt(power + 1e-05)[:, None, None, :]
```

```python
import functools
import math

import jax
import jax.numpy as jnp
import numpy as np
from jax import lax
from jax.experimental import pallas as pl
from jax.experimental.pallas import tpu as pltpu
from jax.sharding import PartitionSpec as P

MESH = pl.DeviceIdType.MESH
RING = 8
ROWS = 4
DIRS = ((1, 0), (0, 1), (-1, 0), (0, -1))
TREE = (
    (2, 2, 2, 2, 2, 2, 2, 2),
    (-1, 1, 1, 1, 1, 1, 3, 3),
    (0, 1, 1, 2, 2, 2, 2, 1),
    (0, 0, 0, 1, 3, 3, 3, 3),
    (0, 0, 0, 1, 1, 0, 3, 3),
    (0, 0, 0, 0, 0, 0, 0, 1),
    (0, 0, 3, 2, 3, 3, 2, 1),
    (2, 0, 3, 2, 0, 0, 2, 0),
)
HOPS = 8
CHUNKS = 8
LAG = 4
SLOTS = CHUNKS + (HOPS - 1) * LAG
SLABS = (0, 1, 3, 2)


def turn(node, times):
    for _ in range(times % 4):
        node = ((-node[1]) % RING, node[0])
    return node


def step_from(node, direction):
    return tuple((node[i] + DIRS[direction][i]) % RING for i in range(2))


def tree_tables():
    def reached(tree, node):
        y, z = turn(node, -tree)
        return -1 if TREE[y][z] < 0 else (TREE[y][z] + tree) % 4

    def depth(tree, node):
        count = 0
        while (link := reached(tree, node)) >= 0:
            node = step_from(node, (link + 2) % 4)
            count += 1
        return count

    table = np.zeros((RING * RING, 8), np.int32)
    for y in range(RING):
        for z in range(RING):
            node = (y, z)
            for tree in range(4):
                link, level = reached(tree, node), depth(tree, node)
                assert level <= HOPS
                start = 0 if level == 0 else CHUNKS + link * SLOTS + (level - 1) * LAG
                table[y * RING + z, 4 + tree] = start
                for out in range(4):
                    if reached(tree, step_from(node, out)) == out:
                        table[y * RING + z, out] = 4 if level == 0 else link
    return table.reshape(-1)


def phase_table(band, lags):
    turns = np.arange(lags)[:, None] - lags // 2
    phase = (turns * np.arange(band)[None, :]) % (2 * band) * (math.pi / band)
    return np.concatenate([np.cos(phase), np.sin(phase)], axis=1).astype(np.float32)


def kernel(
    receivers_ref,
    sources_ref,
    basis_hbm,
    phase_hbm,
    coupling_ref,
    order_ref,
    table_ref,
    out_ref,
    basis_ref,
    phase_ref,
    rx_ref,
    gain_ref,
    taken_ref,
    pick_ref,
    mate_ref,
    block_ref,
    stream_ref,
    send_ref,
    rows_ref,
    result_ref,
    other_ref,
    part_ref,
    near_ref,
    line_ref,
    far_ref,
    local_sem,
    rx_send,
    rx_recv,
    gain_sem,
    one_send,
    one_recv,
    mate_sem,
    x_send,
    x_recv,
    flow_send,
    flow_recv,
    other_sem,
    near_send,
    near_recv,
    far_send,
    far_recv,
):
    chan, me_x = lax.axis_index("chan"), lax.axis_index("win")
    core = chan % 2
    me_y = chan // 2 % RING
    me_z = chan // (2 * RING)

    def at(dy, dz, which, dx=0):
        y, z = (me_y + dy) % RING, (me_z + dz) % RING
        return ((z * RING + y) * 2 + which, (me_x + dx) % ROWS)

    def remote(src, dst, send, recv, device):
        return pltpu.make_async_remote_copy(
            src_ref=src, dst_ref=dst, send_sem=send, recv_sem=recv, device_id=device, device_id_type=MESH
        )

    partner = at(0, 0, 1 - core)
    y_mates = [at(d, 0, core) for d in range(1, RING)]
    z_mates = [at(0, d, which) for which in (core, 1 - core) for d in range(1, RING)]
    x_mates = [at(0, 0, which, d) for which in (core, 1 - core) for d in range(1, ROWS)]
    links = [at(dy, dz, core) for dy, dz in DIRS]

    loads = [
        pltpu.make_async_copy(basis_hbm, basis_ref, local_sem.at[0]),
        pltpu.make_async_copy(phase_hbm, phase_ref, local_sem.at[1]),
        pltpu.make_async_copy(receivers_ref, rx_ref.at[0, core], local_sem.at[2]),
    ]
    for load in loads:
        load.start()
    barrier = pltpu.get_barrier_semaphore()
    greeted = [partner, *y_mates, *z_mates, *x_mates]
    for device in greeted:
        pl.semaphore_signal(barrier, inc=1, device_id=device, device_id_type=MESH)
    for c in range(8):
        gain_ref[core, c : c + 1, :] = jnp.full((1, 128), coupling_ref[c], jnp.float32)
    pl.semaphore_wait(barrier, len(greeted))

    ones = [
        remote(
            sources_ref.at[:, :, pl.ds(128 * link, 128)],
            taken_ref.at[link],
            one_send.at[link],
            one_recv.at[link],
            links[link],
        )
        for link in range(4)
    ]
    for copy in ones:
        copy.start()
    rx = []
    for n, (dx, flip) in enumerate((dx, flip) for flip in (0, 1) for dx in range(ROWS)):
        if n:
            rx.append(
                remote(
                    receivers_ref,
                    rx_ref.at[(ROWS - dx) % ROWS, core],
                    rx_send.at[n],
                    rx_recv.at[n],
                    at(0, 0, core if flip == 0 else 1 - core, dx),
                )
            )
    for copy in rx:
        copy.start()
    gains = remote(gain_ref.at[core], gain_ref.at[core], gain_sem.at[0], gain_sem.at[1], partner)
    gains.start()

    loads[0].wait()
    loads[1].wait()
    tables = lax.dot_general(
        basis_ref[...],
        phase_ref[...],
        (((0,), (0,)), ((), ())),
        precision=lax.Precision.HIGHEST,
        preferred_element_type=jnp.float32,
    )
    band = tables.shape[1] // 2
    cosine, sine = tables[:, :band], tables[:, band:]

    loads[2].wait()
    for copy in rx:
        copy.wait_recv()

    def project(n, carry):
        place, which = n // 2, n % 2
        pair = place // 2
        slab = jnp.where(pair == 2, 3, jnp.where(pair == 3, 2, pair))
        spectra = rx_ref[slab, which, place % 2].astype(jnp.float32)
        for c in range(8):
            real, imag = spectra[c : c + 1, :band], spectra[c : c + 1, band:]
            both = jnp.concatenate([real * cosine - imag * sine, real * sine + imag * cosine], axis=1)
            first = pl.multiple_of(which * 256 + c * 32, 32)
            rows_ref[place, pl.ds(first, 32), :] = both.astype(jnp.bfloat16)
        return carry

    lax.fori_loop(0, 2 * CHUNKS, project, 0)

    owners = [order_ref[b] for b in range(2)]
    roots = [(o // 2 % RING, o // (2 * RING), o % 2) for o in owners]
    relative = [((me_y - y + RING) % RING, (me_z - z + RING) % RING) for y, z, _ in roots]

    for copy in ones:
        copy.wait_recv()
    for b in range(2):
        kept = taken_ref[0]
        for link in range(1, 4):
            dy, dz = DIRS[link]
            here = jnp.logical_and(relative[b][0] == dy % RING, relative[b][1] == dz % RING)
            kept = jnp.where(here, taken_ref[link], kept)
        pick_ref[b] = kept
    mate = remote(pick_ref.at[1 - core], mate_ref, mate_sem.at[0], mate_sem.at[1], partner)
    mate.start()
    mate.wait_recv()
    mine = core == 0
    root_core = jnp.where(mine, roots[0][2], roots[1][2])
    block_ref[...] = jnp.where(root_core == core, pick_ref[core], mate_ref[...])

    crossings = []
    for dx in range(1, ROWS):
        place = SLABS.index((ROWS - dx) % ROWS)
        crossings.append(
            remote(
                block_ref.at[:, pl.ds(pl.multiple_of((me_x + dx) % ROWS * 64, 64), 64), :],
                stream_ref.at[pl.ds(2 * place, 2)],
                x_send.at[dx],
                x_recv.at[dx],
                at(0, 0, core, dx),
            )
        )
    for copy in crossings:
        copy.start()
    stream_ref[0:2] = block_ref[:, pl.ds(pl.multiple_of(me_x * 64, 64), 64), :]

    rel_y = jnp.where(mine, relative[0][0], relative[1][0])
    rel_z = jnp.where(mine, relative[0][1], relative[1][1])
    entry = (rel_y * RING + rel_z) * 8
    forward = [table_ref[entry + link] for link in range(4)]
    start = [table_ref[entry + 4 + tree] for tree in range(4)]

    def flow(link, slot):
        return remote(
            send_ref.at[link * SLOTS + slot],
            stream_ref.at[CHUNKS + link * SLOTS + slot],
            flow_send.at[link * SLOTS + slot],
            flow_recv.at[link * SLOTS + slot],
            links[link],
        )

    def pass_on(slot, own, came):
        heard = [stream_ref[CHUNKS + link * SLOTS + slot - LAG] for link in range(4)] if came else []
        for link in range(4):
            value = own if own is not None else heard[0]
            for n, got in enumerate(heard):
                value = jnp.where(forward[link] == n, got, value)
            send_ref[link * SLOTS + slot] = value
            flow(link, slot).start()

    for slot in range(CHUNKS):
        if slot and slot % 2 == 0:
            crossings[(ROWS - SLABS[slot // 2]) % ROWS - 1].wait_recv()
        if slot >= LAG:
            for link in range(4):
                flow(link, slot - LAG).wait_recv()
        pass_on(slot, stream_ref[slot], slot >= LAG)

    def later(slot, carry):
        for link in range(4):
            flow(link, slot - LAG).wait_recv()
        pass_on(slot, None, True)
        return carry

    lax.fori_loop(CHUNKS, SLOTS, later, 0)
    for slot in range(SLOTS - LAG, SLOTS):
        for link in range(4):
            flow(link, slot).wait_recv()

    total = jnp.zeros(result_ref.shape, jnp.float32)
    for place in range(CHUNKS):
        block = jnp.concatenate([stream_ref[start[tree] + place] for tree in range(4)], axis=1)
        total = total + lax.dot_general(
            rows_ref[place], block, (((1,), (1,)), ((), ())), preferred_element_type=jnp.float32
        )
    gains.wait()
    power = jnp.zeros((8, 64), jnp.float32)
    for c in range(16):
        piece = total[c * 32 : c * 32 + 32] * gain_ref[c // 8, c % 8 : c % 8 + 1, :64]
        result_ref[c * 32 : c * 32 + 32, :] = piece
        squared = piece * piece
        power = power + (squared[0:8] + squared[8:16] + squared[16:24] + squared[24:32])
    part_ref[...] = jnp.concatenate([power, power], axis=1)

    nears = [
        remote(part_ref, near_ref.at[d - 1], near_send.at[d - 1], near_recv.at[d - 1], y_mates[d - 1])
        for d in range(1, RING)
    ]
    for copy in nears:
        copy.start()
    other = remote(
        result_ref.at[pl.ds(pl.multiple_of((1 - core) * 256, 256), 256), :],
        other_ref,
        other_sem.at[0],
        other_sem.at[1],
        partner,
    )
    other.start()
    line = part_ref[...]
    for n, copy in enumerate(nears):
        copy.wait_recv()
        line = line + near_ref[n]
    line_ref[...] = line
    fars = []
    for flip in (0, 1):
        for d in range(RING):
            if d or flip:
                fars.append(
                    remote(
                        line_ref,
                        far_ref.at[flip * RING + d],
                        far_send.at[flip * RING + d],
                        far_recv.at[flip * RING + d],
                        at(0, d, core if flip == 0 else 1 - core),
                    )
                )
    for copy in fars:
        copy.start()

    for copy in [*ones, *rx, mate, *crossings, *nears]:
        copy.wait_send()

    def left(slot, carry):
        for link in range(4):
            flow(link, slot).wait_send()
        return carry

    lax.fori_loop(0, SLOTS, left, 0)
    other.wait()
    for copy in fars:
        copy.wait_recv()
    scale = []
    for flip in (0, 1):
        sums = line_ref[...] if flip == 0 else far_ref[RING]
        for d in range(1, RING):
            sums = sums + far_ref[flip * RING + d]
        power = jnp.sum(sums, axis=0, keepdims=True)[:, :64] / 32768.0
        scale.append(lax.rsqrt(power + 1e-05))
    out_ref[core] = result_ref[pl.ds(pl.multiple_of(core * 256, 256), 256), :] * scale[0]
    out_ref[1 - core] = other_ref[...] * scale[1]
    for copy in fars:
        copy.wait_send()


def per_device(receivers, sources, coupling, lag_basis, source_order):
    lags, basis_count = lag_basis.shape
    bf16, f32 = jnp.bfloat16, jnp.float32
    dma = pltpu.SemaphoreType.DMA
    anywhere = pl.BlockSpec(memory_space=pl.ANY)
    scalars = pl.BlockSpec(memory_space=pltpu.SMEM)
    out = pl.pallas_call(
        kernel,
        out_shape=jax.ShapeDtypeStruct((2, 256, 64), f32),
        in_specs=[anywhere] * 4 + [scalars] * 3,
        out_specs=pl.BlockSpec(memory_space=pltpu.VMEM),
        scratch_shapes=[
            pltpu.VMEM((lags, basis_count), f32),
            pltpu.VMEM((lags, 512), f32),
            pltpu.VMEM((ROWS, 2, 2, 8, 512), bf16),
            pltpu.VMEM((2, 8, 128), f32),
            pltpu.VMEM((4, 2, 256, 128), bf16),
            pltpu.VMEM((2, 2, 256, 128), bf16),
            pltpu.VMEM((2, 256, 128), bf16),
            pltpu.VMEM((2, 256, 128), bf16),
            pltpu.VMEM((CHUNKS + 4 * SLOTS, 64, 128), bf16),
            pltpu.VMEM((4 * SLOTS, 64, 128), bf16),
            pltpu.VMEM((CHUNKS, 512, 512), bf16),
            pltpu.VMEM((512, 64), f32),
            pltpu.VMEM((256, 64), f32),
            pltpu.VMEM((8, 128), f32),
            pltpu.VMEM((RING - 1, 8, 128), f32),
            pltpu.VMEM((8, 128), f32),
            pltpu.VMEM((2 * RING, 8, 128), f32),
            dma((3,)),
            dma((2 * ROWS,)),
            dma((2 * ROWS,)),
            dma((2,)),
            dma((4,)),
            dma((4,)),
            dma((2,)),
            dma((ROWS,)),
            dma((ROWS,)),
            dma((4 * SLOTS,)),
            dma((4 * SLOTS,)),
            dma((2,)),
            dma((RING - 1,)),
            dma((RING - 1,)),
            dma((2 * RING,)),
            dma((2 * RING,)),
        ],
        compiler_params=pltpu.CompilerParams(collective_id=0, has_side_effects=True),
    )(
        receivers,
        sources,
        lag_basis,
        jnp.asarray(phase_table(256, lags)),
        coupling,
        source_order,
        jnp.asarray(tree_tables()),
    )
    return out.reshape(2, 8, 32, 64)


def solution(mesh):
    return jax.shard_map(
        per_device,
        mesh=mesh,
        in_specs=(P("win", "chan", None), P("win", "chan", None), P("chan"), P(), P()),
        out_specs=P(None, "chan", None, "win"),
        check_vma=False,
    )
```

```python
import functools
import math

import jax
import jax.numpy as jnp
import numpy as np
from jax import lax
from jax.experimental import pallas as pl
from jax.experimental.pallas import tpu as pltpu
from jax.sharding import PartitionSpec as P

MESH = pl.DeviceIdType.MESH
RING = 8
ROWS = 4
TURNS = ((1, 0), (0, 1), (-1, 0), (0, -1))
LINKS = TURNS + tuple((2 * y, 2 * z) for y, z in TURNS)
TREES = (
    (
        (2, 6, 2, 2, 2, 2, 2, 2),
        (-1, 1, 5, 5, 5, 7, 7, 3),
        (0, 1, 4, 2, 2, 2, 0, 7),
        (4, 3, 5, 4, 5, 4, 4, 5),
        (0, 3, 0, 0, 0, 0, 0, 2),
        (4, 5, 4, 4, 4, 4, 4, 3),
        (0, 2, 0, 2, 2, 6, 0, 2),
        (3, 6, 7, 6, 6, 5, 5, 6),
    ),
    (
        (6, 1, 6, 6, 6, 6, 7, 6),
        (2, 3, 2, 2, 1, 6, 6, 6),
        (-1, 3, 5, 1, 5, 7, 3, 3),
        (0, 2, 0, 0, 7, 0, 2, 0),
        (4, 1, 4, 5, 7, 3, 7, 5),
        (0, 0, 1, 0, 0, 0, 0, 4),
        (4, 0, 4, 4, 4, 4, 4, 0),
        (6, 3, 6, 1, 5, 2, 4, 4),
    ),
)
HOPS = 4
CHUNKS = 8
LAG = 6
SLOTS = CHUNKS + (HOPS - 1) * LAG
OWN = len(LINKS)
PIECE = (2, ROWS, 32, 128)
SLABS = (0, 1, 3, 2)


def turn(node, times):
    for _ in range(times % 4):
        node = ((-node[1]) % RING, node[0])
    return node


def step_from(node, link, sign=1):
    return tuple((node[i] + sign * LINKS[link][i]) % RING for i in range(2))


def tree_tables():
    def reached(tree, node):
        y, z = turn(node, -tree)
        link = TREES[tree // 4][y][z]
        return -1 if link < 0 else link // 4 * 4 + (link + tree) % 4

    def depth(tree, node):
        count = 0
        while (link := reached(tree, node)) >= 0:
            node = step_from(node, link, -1)
            count += 1
        return count

    table = np.zeros((RING * RING, 3 * OWN), np.int32)
    for y in range(RING):
        for z in range(RING):
            row = table[y * RING + z]
            for tree in range(OWN):
                link, level = reached(tree, (y, z)), depth(tree, (y, z))
                assert level <= HOPS
                row[OWN + tree] = 0 if level == 0 else link * HOPS + level - 1
                row[2 * OWN + tree] = level
                for out in range(OWN):
                    if reached(tree, step_from((y, z), out)) == out:
                        row[out] = OWN if level == 0 else link
    return table.reshape(-1)


def phase_table(band, lags):
    turns = np.arange(lags)[:, None] - lags // 2
    phase = (turns * np.arange(band)[None, :]) % (2 * band) * (math.pi / band)
    return np.concatenate([np.cos(phase), np.sin(phase)], axis=1).astype(np.float32)


def kernel(
    receivers_ref,
    sources_ref,
    basis_hbm,
    phase_hbm,
    coupling_ref,
    order_ref,
    table_ref,
    raw_hbm,
    scale_ref,
    basis_ref,
    phase_ref,
    rx_ref,
    gain_ref,
    taken_ref,
    pick_ref,
    mate_ref,
    block_ref,
    own_ref,
    send_ref,
    rows_ref,
    result_ref,
    other_ref,
    part_ref,
    near_ref,
    line_ref,
    far_ref,
    local_sem,
    rx_send,
    rx_recv,
    gain_sem,
    one_send,
    one_recv,
    mate_sem,
    x_send,
    x_recv,
    flow_send,
    flow_recv,
    other_sem,
    near_send,
    near_recv,
    far_send,
    far_recv,
    raw_sem,
    *came_refs,
):
    chan, me_x = lax.axis_index("chan"), lax.axis_index("win")
    core = chan % 2
    me_y = chan // 2 % RING
    me_z = chan // (2 * RING)

    def at(dy, dz, which, dx=0):
        y, z = (me_y + dy) % RING, (me_z + dz) % RING
        return ((z * RING + y) * 2 + which, (me_x + dx) % ROWS)

    def remote(src, dst, send, recv, device):
        return pltpu.make_async_remote_copy(
            src_ref=src, dst_ref=dst, send_sem=send, recv_sem=recv, device_id=device, device_id_type=MESH
        )

    partner = at(0, 0, 1 - core)
    y_mates = [at(d, 0, core) for d in range(1, RING)]
    z_mates = [at(0, d, which) for which in (core, 1 - core) for d in range(1, RING)]
    x_mates = [at(0, 0, which, d) for which in (core, 1 - core) for d in range(1, ROWS)]
    links = [at(dy, dz, core) for dy, dz in LINKS]

    loads = [
        pltpu.make_async_copy(basis_hbm, basis_ref, local_sem.at[0]),
        pltpu.make_async_copy(phase_hbm, phase_ref, local_sem.at[1]),
        pltpu.make_async_copy(receivers_ref, rx_ref.at[0, core], local_sem.at[2]),
    ]
    for load in loads:
        load.start()
    barrier = pltpu.get_barrier_semaphore()
    greeted = [partner, *y_mates, *z_mates, *x_mates]
    for device in greeted:
        pl.semaphore_signal(barrier, inc=1, device_id=device, device_id_type=MESH)
    for c in range(8):
        gain_ref[core, c : c + 1, :] = jnp.full((1, 128), coupling_ref[c], jnp.float32)
    pl.semaphore_wait(barrier, len(greeted))

    ones = [
        remote(
            sources_ref.at[:, :, tree // 4, :, pl.ds(128 * (tree % 4), 128)],
            taken_ref.at[tree],
            one_send.at[tree],
            one_recv.at[tree],
            links[tree],
        )
        for tree in range(OWN)
    ]
    for copy in ones:
        copy.start()
    rx = []
    for n, (dx, flip) in enumerate((dx, flip) for flip in (0, 1) for dx in range(ROWS)):
        if n:
            rx.append(
                remote(
                    receivers_ref,
                    rx_ref.at[(ROWS - dx) % ROWS, core],
                    rx_send.at[n],
                    rx_recv.at[n],
                    at(0, 0, core if flip == 0 else 1 - core, dx),
                )
            )
    for copy in rx:
        copy.start()
    gains = remote(gain_ref.at[core], gain_ref.at[core], gain_sem.at[0], gain_sem.at[1], partner)
    gains.start()

    loads[0].wait()
    loads[1].wait()
    tables = lax.dot_general(
        basis_ref[...],
        phase_ref[...],
        (((1,), (0,)), ((), ())),
        precision=lax.Precision.HIGHEST,
        preferred_element_type=jnp.float32,
    )
    band = tables.shape[1] // 2
    cosine, sine = tables[:, :band], tables[:, band:]

    loads[2].wait()
    for copy in rx:
        copy.wait_recv()

    def project(n, carry):
        place, which = n // 2, n % 2
        pair = place // 2
        slab = jnp.where(pair == 2, 3, jnp.where(pair == 3, 2, pair))
        spectra = rx_ref[slab, which, place % 2].astype(jnp.float32)
        for c in range(8):
            real, imag = spectra[c : c + 1, :band], spectra[c : c + 1, band:]
            both = jnp.concatenate([real * cosine - imag * sine, real * sine + imag * cosine], axis=1)
            first = pl.multiple_of(which * 256 + c * 32, 32)
            rows_ref[place, pl.ds(first, 32), :] = both.astype(jnp.bfloat16)
        return carry

    lax.fori_loop(0, 2 * CHUNKS, project, 0)

    owners = [order_ref[b] for b in range(2)]
    roots = [(o // 2 % RING, o // (2 * RING), o % 2) for o in owners]
    relative = [((me_y - y + RING) % RING, (me_z - z + RING) % RING) for y, z, _ in roots]

    for copy in ones:
        copy.wait_recv()
    for b in range(2):
        kept = taken_ref[0]
        for tree in range(1, OWN):
            dy, dz = LINKS[tree]
            here = jnp.logical_and(relative[b][0] == dy % RING, relative[b][1] == dz % RING)
            kept = jnp.where(here, taken_ref[tree], kept)
        pick_ref[b] = kept
    mate = remote(pick_ref.at[1 - core], mate_ref, mate_sem.at[0], mate_sem.at[1], partner)
    mate.start()
    mate.wait_recv()
    mine = core == 0
    root_core = jnp.where(mine, roots[0][2], roots[1][2])
    block_ref[...] = jnp.where(root_core == core, pick_ref[core], mate_ref[...])

    crossings = []
    for dx in range(1, ROWS):
        place = SLABS.index((ROWS - dx) % ROWS)
        crossings.append(
            remote(
                block_ref.at[:, (me_x + dx) % ROWS],
                own_ref.at[pl.ds(2 * place, 2)],
                x_send.at[dx],
                x_recv.at[dx],
                at(0, 0, core, dx),
            )
        )
    for copy in crossings:
        copy.start()
    own_ref[0:2] = block_ref[:, me_x]

    rel_y = jnp.where(mine, relative[0][0], relative[1][0])
    rel_z = jnp.where(mine, relative[0][1], relative[1][1])
    entry = (rel_y * RING + rel_z) * 3 * OWN
    forward = [table_ref[entry + link] for link in range(OWN)]
    place_of = [table_ref[entry + OWN + tree] for tree in range(OWN)]
    level_of = [table_ref[entry + 2 * OWN + tree] for tree in range(OWN)]

    def landing(link, hop, lane):
        if isinstance(hop, int) and hop == HOPS:
            return came_refs[LAG + lane].at[link]
        return came_refs[lane].at[link * HOPS + hop]

    def flow(link, hop, lane, leaving=False):
        number = link * SLOTS + hop * LAG + lane
        return remote(
            send_ref.at[number],
            came_refs[0].at[0] if leaving else landing(link, hop, lane),
            flow_send.at[number],
            flow_recv.at[number],
            links[link],
        )

    def pass_on(hop, lane, own):
        heard = []
        if not (isinstance(hop, int) and hop == 0):
            for link in range(OWN):
                flow(link, hop - 1, lane).wait_recv()
            heard = [came_refs[lane][link * HOPS + hop - 1] for link in range(OWN)]
        for link in range(OWN):
            value = heard[0] if own is None else own
            for n, got in enumerate(heard):
                value = jnp.where(forward[link] == n, got, value)
            send_ref[link * SLOTS + hop * LAG + lane] = value
            flow(link, hop, lane).start()

    for slot in range(CHUNKS):
        if slot and slot % 2 == 0:
            crossings[(ROWS - SLABS[slot // 2]) % ROWS - 1].wait_recv()
        pass_on(slot // LAG, slot % LAG, own_ref[slot])
    for lane in range(CHUNKS - LAG, LAG):
        pass_on(1, lane, None)

    def later(hop, carry):
        for lane in range(LAG):
            pass_on(hop, lane, None)
        return carry

    lax.fori_loop(2, HOPS, later, 0)
    for lane in range(CHUNKS - LAG):
        pass_on(HOPS, lane, None)

    for chunk in range(CHUNKS):
        late, lane = divmod(chunk, LAG)
        for link in range(OWN):
            if late:
                flow(link, HOPS, lane).wait_recv()
            elif lane >= CHUNKS - LAG:
                flow(link, HOPS - 1, lane).wait_recv()
        halves = []
        for half in range(2):
            pieces = []
            for tree in range(4 * half, 4 * half + 4):
                if late:
                    last = level_of[tree] == HOPS
                    got = came_refs[lane][place_of[tree] + jnp.where(last, 0, 1)]
                    got = jnp.where(last, came_refs[LAG + lane][place_of[tree] // HOPS], got)
                else:
                    got = came_refs[lane][place_of[tree]]
                pieces.append(jnp.where(level_of[tree] == 0, own_ref[chunk], got))
            halves.append(jnp.concatenate(pieces, axis=1))
        product = lax.dot_general(
            rows_ref[chunk],
            jnp.concatenate(halves, axis=0),
            (((1,), (1,)), ((), ())),
            preferred_element_type=jnp.float32,
        )
        if chunk == 0:
            result_ref[...] = product
        else:
            result_ref[...] += product
    gains.wait()
    power = jnp.zeros((8, 64), jnp.float32)
    for c in range(16):
        piece = result_ref[c * 32 : c * 32 + 32, :] * gain_ref[c // 8, c % 8 : c % 8 + 1, :64]
        result_ref[c * 32 : c * 32 + 32, :] = piece
        squared = piece * piece
        power = power + (squared[0:8] + squared[8:16] + squared[16:24] + squared[24:32])
    part_ref[...] = jnp.concatenate([power, power], axis=1)

    nears = [
        remote(part_ref, near_ref.at[d - 1], near_send.at[d - 1], near_recv.at[d - 1], y_mates[d - 1])
        for d in range(1, RING)
    ]
    for copy in nears:
        copy.start()
    other = remote(
        result_ref.at[pl.ds(pl.multiple_of((1 - core) * 256, 256), 256), :],
        other_ref,
        other_sem.at[0],
        other_sem.at[1],
        partner,
    )
    other.start()
    line = part_ref[...]
    for n, copy in enumerate(nears):
        copy.wait_recv()
        line = line + near_ref[n]
    line_ref[...] = line
    fars = []
    for flip in (0, 1):
        for d in range(RING):
            if d or flip:
                fars.append(
                    remote(
                        line_ref,
                        far_ref.at[flip * RING + d],
                        far_send.at[flip * RING + d],
                        far_recv.at[flip * RING + d],
                        at(0, d, core if flip == 0 else 1 - core),
                    )
                )
    for copy in fars:
        copy.start()

    for copy in [*ones, *rx, mate, *crossings, *nears]:
        copy.wait_send()

    def left(slot, carry):
        for link in range(OWN):
            flow(link, 0, slot, True).wait_send()
        return carry

    lax.fori_loop(0, SLOTS, left, 0)
    other.wait()
    writes = [
        pltpu.make_async_copy(
            result_ref.at[pl.ds(pl.multiple_of(core * 256, 256), 256), :], raw_hbm.at[core], raw_sem.at[0]
        ),
        pltpu.make_async_copy(other_ref, raw_hbm.at[1 - core], raw_sem.at[1]),
    ]
    for write in writes:
        write.start()
    for copy in fars:
        copy.wait_recv()
    for flip in (0, 1):
        sums = line_ref[...] if flip == 0 else far_ref[RING]
        for d in range(1, RING):
            sums = sums + far_ref[flip * RING + d]
        power = jnp.sum(sums, axis=0, keepdims=True)[:, :64] / 32768.0
        scale_ref[core if flip == 0 else 1 - core] = lax.rsqrt(power + 1e-05)
    for write in writes:
        write.wait()
    for copy in fars:
        copy.wait_send()


def per_device(receivers, sources, coupling, lag_basis, source_order):
    lags, basis_count = lag_basis.shape
    bf16, f32 = jnp.bfloat16, jnp.float32
    dma = pltpu.SemaphoreType.DMA
    anywhere = pl.BlockSpec(memory_space=pl.ANY)
    scalars = pl.BlockSpec(memory_space=pltpu.SMEM)
    raw, scale = pl.pallas_call(
        kernel,
        out_shape=(jax.ShapeDtypeStruct((2, 256, 64), f32), jax.ShapeDtypeStruct((2, 1, 64), f32)),
        in_specs=[anywhere] * 4 + [scalars] * 3,
        out_specs=(anywhere, pl.BlockSpec(memory_space=pltpu.VMEM)),
        scratch_shapes=[
            pltpu.VMEM((basis_count, lags), f32),
            pltpu.VMEM((lags, 512), f32),
            pltpu.VMEM((ROWS, 2, 2, 8, 512), bf16),
            pltpu.VMEM((2, 8, 128), f32),
            pltpu.VMEM((OWN, *PIECE), bf16),
            pltpu.VMEM((2, *PIECE), bf16),
            pltpu.VMEM(PIECE, bf16),
            pltpu.VMEM(PIECE, bf16),
            pltpu.VMEM((CHUNKS, 32, 128), bf16),
            pltpu.VMEM((OWN * SLOTS, 32, 128), bf16),
            pltpu.VMEM((CHUNKS, 512, 512), bf16),
            pltpu.VMEM((512, 64), f32),
            pltpu.VMEM((256, 64), f32),
            pltpu.VMEM((8, 128), f32),
            pltpu.VMEM((RING - 1, 8, 128), f32),
            pltpu.VMEM((8, 128), f32),
            pltpu.VMEM((2 * RING, 8, 128), f32),
            dma((3,)),
            dma((2 * ROWS,)),
            dma((2 * ROWS,)),
            dma((2,)),
            dma((OWN,)),
            dma((OWN,)),
            dma((2,)),
            dma((ROWS,)),
            dma((ROWS,)),
            dma((OWN * SLOTS,)),
            dma((OWN * SLOTS,)),
            dma((2,)),
            dma((RING - 1,)),
            dma((RING - 1,)),
            dma((2 * RING,)),
            dma((2 * RING,)),
            dma((2,)),
            *[pltpu.VMEM((OWN * HOPS, 32, 128), bf16)] * LAG,
            *[pltpu.VMEM((OWN, 32, 128), bf16)] * (CHUNKS - LAG),
        ],
        compiler_params=pltpu.CompilerParams(collective_id=0, has_side_effects=True),
    )(
        receivers,
        sources.reshape(2, ROWS, 2, 32, 512),
        lag_basis.T,
        jnp.asarray(phase_table(256, lags)),
        coupling,
        source_order,
        jnp.asarray(tree_tables()),
    )
    return raw.reshape(2, 8, 32, 64) * scale[:, None]


def solution(mesh):
    return jax.shard_map(
        per_device,
        mesh=mesh,
        in_specs=(P("win", "chan", None), P("win", "chan", None), P("chan"), P(), P()),
        out_specs=P(None, "chan", None, "win"),
        check_vma=False,
    )
```

```python
import functools
import math

import jax
import jax.numpy as jnp
import numpy as np
from jax import lax
from jax.experimental import pallas as pl
from jax.experimental.pallas import tpu as pltpu
from jax.sharding import PartitionSpec as P

MESH = pl.DeviceIdType.MESH
RING = 8
ROWS = 4
TURNS = ((1, 0), (0, 1), (-1, 0), (0, -1))
LINKS = TURNS + tuple((2 * y, 2 * z) for y, z in TURNS)
TREES = (
    (
        (2, 6, 2, 2, 2, 2, 2, 2),
        (-1, 1, 5, 5, 5, 7, 7, 3),
        (0, 1, 4, 2, 2, 2, 0, 7),
        (4, 3, 5, 4, 5, 4, 4, 5),
        (0, 3, 0, 0, 0, 0, 0, 2),
        (4, 5, 4, 4, 4, 4, 4, 3),
        (0, 2, 0, 2, 2, 6, 0, 2),
        (3, 6, 7, 6, 6, 5, 5, 6),
    ),
    (
        (6, 1, 6, 6, 6, 6, 7, 6),
        (2, 3, 2, 2, 1, 6, 6, 6),
        (-1, 3, 5, 1, 5, 7, 3, 3),
        (0, 2, 0, 0, 7, 0, 2, 0),
        (4, 1, 4, 5, 7, 3, 7, 5),
        (0, 0, 1, 0, 0, 0, 0, 4),
        (4, 0, 4, 4, 4, 4, 4, 0),
        (6, 3, 6, 1, 5, 2, 4, 4),
    ),
)
HOPS = 4
CHUNKS = 2 * ROWS
LAG = 6
SLOTS = CHUNKS + (HOPS - 1) * LAG
OWN = len(LINKS)
PIECE = (ROWS, 32, 128)
SLABS = (0, 1, 3, 2)


def turn(node, times):
    for _ in range(times % 4):
        node = ((-node[1]) % RING, node[0])
    return node


def step_from(node, link, sign=1):
    return tuple((node[i] + sign * LINKS[link][i]) % RING for i in range(2))


def tree_tables():
    def reached(tree, node):
        y, z = turn(node, -tree)
        link = TREES[tree // 4][y][z]
        return -1 if link < 0 else link // 4 * 4 + (link + tree) % 4

    def depth(tree, node):
        count = 0
        while (link := reached(tree, node)) >= 0:
            node = step_from(node, link, -1)
            count += 1
        return count

    table = np.zeros((RING * RING, 3 * OWN), np.int32)
    for y in range(RING):
        for z in range(RING):
            row = table[y * RING + z]
            for tree in range(OWN):
                link, level = reached(tree, (y, z)), depth(tree, (y, z))
                assert level <= HOPS
                row[OWN + tree] = 0 if level == 0 else link * HOPS + level - 1
                row[2 * OWN + tree] = level
                for out in range(OWN):
                    if reached(tree, step_from((y, z), out)) == out:
                        row[out] = OWN if level == 0 else link
    return table.reshape(-1)


def phase_table(band, lags):
    turns = np.arange(lags)[:, None] - lags // 2
    phase = (turns * np.arange(band)[None, :]) % (2 * band) * (math.pi / band)
    return np.concatenate([np.cos(phase), np.sin(phase)], axis=1).astype(np.float32)


def kernel(
    receivers_ref,
    sources_ref,
    basis_hbm,
    phase_hbm,
    coupling_ref,
    order_ref,
    table_ref,
    raw_hbm,
    basis_ref,
    phase_ref,
    rx_ref,
    gain_ref,
    taken_ref,
    pick_ref,
    both_ref,
    own_ref,
    send_ref,
    rows_ref,
    result_ref,
    other_ref,
    part_ref,
    near_ref,
    line_ref,
    far_ref,
    scale_ref,
    local_sem,
    rx_send,
    rx_recv,
    gain_sem,
    one_send,
    one_recv,
    x_send,
    x_recv,
    flow_send,
    flow_recv,
    other_sem,
    near_send,
    near_recv,
    far_send,
    far_recv,
    raw_sem,
    *came_refs,
):
    chan, me_x = lax.axis_index("chan"), lax.axis_index("win")
    core = chan % 2
    me_y = chan // 2 % RING
    me_z = chan // (2 * RING)

    def at(dy, dz, which, dx=0):
        y, z = (me_y + dy) % RING, (me_z + dz) % RING
        return ((z * RING + y) * 2 + which, (me_x + dx) % ROWS)

    def remote(src, dst, send, recv, device):
        return pltpu.make_async_remote_copy(
            src_ref=src, dst_ref=dst, send_sem=send, recv_sem=recv, device_id=device, device_id_type=MESH
        )

    partner = at(0, 0, 1 - core)
    y_mates = [at(d, 0, core) for d in range(1, RING)]
    z_mates = [at(0, d, which) for which in (core, 1 - core) for d in range(1, RING)]
    x_mates = [at(0, 0, which, d) for which in (core, 1 - core) for d in range(1, ROWS)]
    links = [at(dy, dz, core) for dy, dz in LINKS]

    loads = [
        pltpu.make_async_copy(basis_hbm, basis_ref, local_sem.at[0]),
        pltpu.make_async_copy(phase_hbm, phase_ref, local_sem.at[1]),
        pltpu.make_async_copy(receivers_ref, rx_ref.at[0, core], local_sem.at[2]),
    ]
    for load in loads:
        load.start()
    barrier = pltpu.get_barrier_semaphore()
    greeted = [partner, *y_mates, *z_mates, *x_mates]
    for device in greeted:
        pl.semaphore_signal(barrier, inc=1, device_id=device, device_id_type=MESH)
    for c in range(8):
        gain_ref[core, c : c + 1, :] = jnp.full((1, 128), coupling_ref[c], jnp.float32)
    pl.semaphore_wait(barrier, len(greeted))

    ones = [
        remote(
            sources_ref.at[half, :, tree // 4, :, pl.ds(128 * (tree % 4), 128)],
            taken_ref.at[half, tree],
            one_send.at[half * OWN + tree],
            one_recv.at[half * OWN + tree],
            links[tree],
        )
        for half in range(2)
        for tree in range(OWN)
    ]
    for copy in ones:
        copy.start()
    rx = []
    for n, (dx, flip) in enumerate((dx, flip) for flip in (0, 1) for dx in range(ROWS)):
        if n:
            rx.append(
                remote(
                    receivers_ref,
                    rx_ref.at[(ROWS - dx) % ROWS, core],
                    rx_send.at[n],
                    rx_recv.at[n],
                    at(0, 0, core if flip == 0 else 1 - core, dx),
                )
            )
    for copy in rx:
        copy.start()
    gains = remote(gain_ref.at[core], gain_ref.at[core], gain_sem.at[0], gain_sem.at[1], partner)
    gains.start()

    loads[0].wait()
    loads[1].wait()
    tables = lax.dot_general(
        basis_ref[...],
        phase_ref[...],
        (((1,), (0,)), ((), ())),
        precision=lax.Precision.HIGHEST,
        preferred_element_type=jnp.float32,
    )
    band = tables.shape[1] // 2
    cosine, sine = tables[:, :band], tables[:, band:]

    loads[2].wait()
    for copy in rx:
        copy.wait_recv()

    def project(n, carry):
        place, which = n // 2, n % 2
        turned = place % ROWS
        slab = jnp.where(turned == 2, 3, jnp.where(turned == 3, 2, turned))
        spectra = rx_ref[slab, which, place // ROWS].astype(jnp.float32)
        for c in range(8):
            real, imag = spectra[c : c + 1, :band], spectra[c : c + 1, band:]
            both = jnp.concatenate([real * cosine - imag * sine, real * sine + imag * cosine], axis=1)
            first = pl.multiple_of(which * 256 + c * 32, 32)
            rows_ref[place, pl.ds(first, 32), :] = both.astype(jnp.bfloat16)
        return carry

    lax.fori_loop(0, 2 * CHUNKS, project, 0)

    owners = [order_ref[b] for b in range(2)]
    roots = [(o // 2 % RING, o // (2 * RING), o % 2) for o in owners]
    relative = [((me_y - y + RING) % RING, (me_z - z + RING) % RING) for y, z, _ in roots]

    crossings = []
    for half in range(2):
        for tree in range(OWN):
            ones[half * OWN + tree].wait_recv()
        for b in range(2):
            kept = taken_ref[half, 0]
            for tree in range(1, OWN):
                dy, dz = LINKS[tree]
                here = jnp.logical_and(relative[b][0] == dy % RING, relative[b][1] == dz % RING)
                kept = jnp.where(here, taken_ref[half, tree], kept)
            pick_ref[half, b] = kept
        for n in range(1, 2 * ROWS):
            flip, dx = divmod(n, ROWS)
            which = core if flip == 0 else 1 - core
            place = half * ROWS + SLABS.index((ROWS - dx) % ROWS)
            crossings.append(
                remote(
                    pick_ref.at[half, which, (me_x + dx) % ROWS],
                    both_ref.at[core, place],
                    x_send.at[half * 2 * ROWS + n],
                    x_recv.at[half * 2 * ROWS + n],
                    at(0, 0, which, dx),
                )
            )
            crossings[-1].start()
        both_ref[core, half * ROWS] = pick_ref[half, core, me_x]
    mine = core == 0
    root_core = jnp.where(mine, roots[0][2], roots[1][2])

    rel_y = jnp.where(mine, relative[0][0], relative[1][0])
    rel_z = jnp.where(mine, relative[0][1], relative[1][1])
    entry = (rel_y * RING + rel_z) * 3 * OWN
    forward = [table_ref[entry + link] for link in range(OWN)]
    place_of = [table_ref[entry + OWN + tree] for tree in range(OWN)]
    level_of = [table_ref[entry + 2 * OWN + tree] for tree in range(OWN)]

    def landing(link, hop, lane):
        if isinstance(hop, int) and hop == HOPS:
            return came_refs[LAG + lane].at[link]
        return came_refs[lane].at[link * HOPS + hop]

    def flow(link, hop, lane, leaving=False):
        number = link * SLOTS + hop * LAG + lane
        return remote(
            send_ref.at[number],
            came_refs[0].at[0] if leaving else landing(link, hop, lane),
            flow_send.at[number],
            flow_recv.at[number],
            links[link],
        )

    def pass_on(hop, lane, own):
        heard = []
        if not (isinstance(hop, int) and hop == 0):
            for link in range(OWN):
                flow(link, hop - 1, lane).wait_recv()
            heard = [came_refs[lane][link * HOPS + hop - 1] for link in range(OWN)]
        for link in range(OWN):
            value = heard[0] if own is None else own
            for n, got in enumerate(heard):
                value = jnp.where(forward[link] == n, got, value)
            send_ref[link * SLOTS + hop * LAG + lane] = value
            flow(link, hop, lane).start()

    for slot in range(CHUNKS):
        half, place = divmod(slot, ROWS)
        dx = (ROWS - SLABS[place]) % ROWS
        for n in (dx, ROWS + dx):
            if n:
                crossings[half * (2 * ROWS - 1) + n - 1].wait_recv()
        own = jnp.where(root_core == 0, both_ref[0, slot], both_ref[1, slot])
        own_ref[slot] = own
        pass_on(slot // LAG, slot % LAG, own)
    for lane in range(CHUNKS - LAG, LAG):
        pass_on(1, lane, None)

    def later(hop, carry):
        for lane in range(LAG):
            pass_on(hop, lane, None)
        return carry

    lax.fori_loop(2, HOPS, later, 0)
    for lane in range(CHUNKS - LAG):
        pass_on(HOPS, lane, None)

    for chunk in range(CHUNKS):
        late, lane = divmod(chunk, LAG)
        for link in range(OWN):
            if late:
                flow(link, HOPS, lane).wait_recv()
            elif lane >= CHUNKS - LAG:
                flow(link, HOPS - 1, lane).wait_recv()
        halves = []
        for half in range(2):
            pieces = []
            for tree in range(4 * half, 4 * half + 4):
                if late:
                    last = level_of[tree] == HOPS
                    got = came_refs[lane][place_of[tree] + jnp.where(last, 0, 1)]
                    got = jnp.where(last, came_refs[LAG + lane][place_of[tree] // HOPS], got)
                else:
                    got = came_refs[lane][place_of[tree]]
                pieces.append(jnp.where(level_of[tree] == 0, own_ref[chunk], got))
            halves.append(jnp.concatenate(pieces, axis=1))
        product = lax.dot_general(
            rows_ref[chunk],
            jnp.concatenate(halves, axis=0),
            (((1,), (1,)), ((), ())),
            preferred_element_type=jnp.float32,
        )
        product = product.reshape(16, 32, 64)
        if chunk == 0:
            result_ref[...] = product
        else:
            result_ref[...] += product
    gains.wait()
    power = jnp.zeros((32, 64), jnp.float32)
    for c in range(16):
        piece = result_ref[c] * gain_ref[c // 8, c % 8 : c % 8 + 1, :64]
        result_ref[c] = piece
        power = power + piece * piece
    power = jnp.sum(power, axis=0, keepdims=True)
    part_ref[...] = jnp.concatenate([power, power], axis=1)

    nears = [
        remote(part_ref, near_ref.at[d - 1], near_send.at[d - 1], near_recv.at[d - 1], y_mates[d - 1])
        for d in range(1, RING)
    ]
    for copy in nears:
        copy.start()
    other = remote(
        result_ref.at[pl.ds((1 - core) * 8, 8)],
        other_ref,
        other_sem.at[0],
        other_sem.at[1],
        partner,
    )
    other.start()
    line = part_ref[...]
    for n, copy in enumerate(nears):
        copy.wait_recv()
        line = line + near_ref[n]
    line_ref[...] = line
    fars = []
    for flip in (0, 1):
        for d in range(RING):
            if d or flip:
                fars.append(
                    remote(
                        line_ref,
                        far_ref.at[flip * RING + d],
                        far_send.at[flip * RING + d],
                        far_recv.at[flip * RING + d],
                        at(0, d, core if flip == 0 else 1 - core),
                    )
                )
    for copy in fars:
        copy.start()

    for copy in [*ones, *rx, *crossings, *nears]:
        copy.wait_send()

    def left(slot, carry):
        for link in range(OWN):
            flow(link, 0, slot, True).wait_send()
        return carry

    lax.fori_loop(0, SLOTS, left, 0)
    other.wait()
    writes = [
        pltpu.make_async_copy(
            result_ref.at[pl.ds(core * 8, 8)], raw_hbm.at[core, pl.ds(0, 8)], raw_sem.at[0]
        ),
        pltpu.make_async_copy(other_ref, raw_hbm.at[1 - core, pl.ds(0, 8)], raw_sem.at[1]),
    ]
    for write in writes:
        write.start()
    for copy in fars:
        copy.wait_recv()
    for flip in (0, 1):
        sums = line_ref[...] if flip == 0 else far_ref[RING]
        for d in range(1, RING):
            sums = sums + far_ref[flip * RING + d]
        scale = lax.rsqrt(sums[:, :64] / 32768.0 + 1e-05)
        scale_ref[core if flip == 0 else 1 - core] = jnp.broadcast_to(scale, (8, 64))
    last = pltpu.make_async_copy(scale_ref, raw_hbm.at[:, 8, pl.ds(0, 8)], raw_sem.at[2])
    last.start()
    writes.append(last)
    for write in writes:
        write.wait()
    for copy in fars:
        copy.wait_send()


def per_device(receivers, sources, coupling, lag_basis, source_order):
    lags, basis_count = lag_basis.shape
    bf16, f32 = jnp.bfloat16, jnp.float32
    dma = pltpu.SemaphoreType.DMA
    anywhere = pl.BlockSpec(memory_space=pl.ANY)
    scalars = pl.BlockSpec(memory_space=pltpu.SMEM)
    raw = pl.pallas_call(
        kernel,
        out_shape=jax.ShapeDtypeStruct((2, 9, 32, 64), f32),
        in_specs=[anywhere] * 4 + [scalars] * 3,
        out_specs=anywhere,
        scratch_shapes=[
            pltpu.VMEM((basis_count, lags), f32),
            pltpu.VMEM((lags, 512), f32),
            pltpu.VMEM((ROWS, 2, 2, 8, 512), bf16),
            pltpu.VMEM((2, 8, 128), f32),
            pltpu.VMEM((2, OWN, *PIECE), bf16),
            pltpu.VMEM((2, 2, *PIECE), bf16),
            pltpu.VMEM((2, CHUNKS, 32, 128), bf16),
            pltpu.VMEM((CHUNKS, 32, 128), bf16),
            pltpu.VMEM((OWN * SLOTS, 32, 128), bf16),
            pltpu.VMEM((CHUNKS, 512, 512), bf16),
            pltpu.VMEM((16, 32, 64), f32),
            pltpu.VMEM((8, 32, 64), f32),
            pltpu.VMEM((1, 128), f32),
            pltpu.VMEM((RING - 1, 1, 128), f32),
            pltpu.VMEM((1, 128), f32),
            pltpu.VMEM((2 * RING, 1, 128), f32),
            pltpu.VMEM((2, 8, 64), f32),
            dma((3,)),
            dma((2 * ROWS,)),
            dma((2 * ROWS,)),
            dma((2,)),
            dma((2 * OWN,)),
            dma((2 * OWN,)),
            dma((4 * ROWS,)),
            dma((4 * ROWS,)),
            dma((OWN * SLOTS,)),
            dma((OWN * SLOTS,)),
            dma((2,)),
            dma((RING - 1,)),
            dma((RING - 1,)),
            dma((2 * RING,)),
            dma((2 * RING,)),
            dma((3,)),
            *[pltpu.VMEM((OWN * HOPS, 32, 128), bf16)] * LAG,
            *[pltpu.VMEM((OWN, 32, 128), bf16)] * (CHUNKS - LAG),
        ],
        compiler_params=pltpu.CompilerParams(collective_id=0, has_side_effects=True),
    )(
        receivers,
        sources.reshape(2, ROWS, 2, 32, 512),
        lag_basis.T,
        jnp.asarray(phase_table(256, lags)),
        coupling,
        source_order,
        jnp.asarray(tree_tables()),
    )
    return raw[:, :8] * raw[:, 8:, :1]


def solution(mesh):
    return jax.shard_map(
        per_device,
        mesh=mesh,
        in_specs=(P("win", "chan", None), P("win", "chan", None), P("chan"), P(), P()),
        out_specs=P(None, "chan", None, "win"),
        check_vma=False,
    )
```

```python
import functools
import math

import jax
import jax.numpy as jnp
import numpy as np
from jax import lax
from jax.experimental import pallas as pl
from jax.experimental.pallas import tpu as pltpu
from jax.sharding import PartitionSpec as P

MESH = pl.DeviceIdType.MESH
RING = 8
ROWS = 4
TURNS = ((1, 0), (0, 1), (-1, 0), (0, -1))
LINKS = TURNS + tuple((2 * y, 2 * z) for y, z in TURNS)
TREES = (
    (
        (2, 6, 2, 2, 2, 2, 2, 2),
        (-1, 1, 5, 5, 5, 7, 7, 3),
        (0, 1, 4, 2, 2, 2, 0, 7),
        (4, 3, 5, 4, 5, 4, 4, 5),
        (0, 3, 0, 0, 0, 0, 0, 2),
        (4, 5, 4, 4, 4, 4, 4, 3),
        (0, 2, 0, 2, 2, 6, 0, 2),
        (3, 6, 7, 6, 6, 5, 5, 6),
    ),
    (
        (6, 1, 6, 6, 6, 6, 7, 6),
        (2, 3, 2, 2, 1, 6, 6, 6),
        (-1, 3, 5, 1, 5, 7, 3, 3),
        (0, 2, 0, 0, 7, 0, 2, 0),
        (4, 1, 4, 5, 7, 3, 7, 5),
        (0, 0, 1, 0, 0, 0, 0, 4),
        (4, 0, 4, 4, 4, 4, 4, 0),
        (6, 3, 6, 1, 5, 2, 4, 4),
    ),
)
HOPS = 4
CHUNKS = 2 * ROWS
LAG = 6
SLOTS = CHUNKS + (HOPS - 1) * LAG
OWN = len(LINKS)
PIECE = (ROWS, 32, 128)
SLABS = (0, 1, 3, 2)


def turn(node, times):
    for _ in range(times % 4):
        node = ((-node[1]) % RING, node[0])
    return node


def step_from(node, link, sign=1):
    return tuple((node[i] + sign * LINKS[link][i]) % RING for i in range(2))


def tree_tables():
    def reached(tree, node):
        y, z = turn(node, -tree)
        link = TREES[tree // 4][y][z]
        return -1 if link < 0 else link // 4 * 4 + (link + tree) % 4

    def depth(tree, node):
        count = 0
        while (link := reached(tree, node)) >= 0:
            node = step_from(node, link, -1)
            count += 1
        return count

    table = np.zeros((RING * RING, 3 * OWN), np.int32)
    for y in range(RING):
        for z in range(RING):
            row = table[y * RING + z]
            for tree in range(OWN):
                link, level = reached(tree, (y, z)), depth(tree, (y, z))
                assert level <= HOPS
                row[OWN + tree] = 0 if level == 0 else link * HOPS + level - 1
                row[2 * OWN + tree] = level
                for out in range(OWN):
                    if reached(tree, step_from((y, z), out)) == out:
                        row[out] = OWN if level == 0 else link
    return table.reshape(-1)


def phase_table(band, lags):
    turns = np.arange(lags)[:, None] - lags // 2
    phase = (turns * np.arange(band)[None, :]) % (2 * band) * (math.pi / band)
    return np.concatenate([np.cos(phase), np.sin(phase)], axis=1).astype(np.float32)


def kernel(
    receivers_ref,
    sources_ref,
    basis_hbm,
    phase_hbm,
    coupling_hbm,
    order_hbm,
    table_hbm,
    out_ref,
    coupling_ref,
    order_ref,
    table_ref,
    basis_ref,
    phase_ref,
    rx_ref,
    gain_ref,
    taken_ref,
    pick_ref,
    both_ref,
    own_ref,
    send_ref,
    rows_ref,
    result_ref,
    other_ref,
    part_ref,
    plane_ref,
    sum_ref,
    mate_ref,
    local_sem,
    rx_send,
    rx_recv,
    gain_sem,
    one_send,
    one_recv,
    x_send,
    x_recv,
    flow_send,
    flow_recv,
    other_sem,
    plane_send,
    plane_recv,
    mate_sem,
    *came_refs,
):
    chan, me_x = lax.axis_index("chan"), lax.axis_index("win")
    core = chan % 2
    me_y = chan // 2 % RING
    me_z = chan // (2 * RING)

    def at(dy, dz, which, dx=0):
        y, z = (me_y + dy) % RING, (me_z + dz) % RING
        return ((z * RING + y) * 2 + which, (me_x + dx) % ROWS)

    def remote(src, dst, send, recv, device):
        return pltpu.make_async_remote_copy(
            src_ref=src, dst_ref=dst, send_sem=send, recv_sem=recv, device_id=device, device_id_type=MESH
        )

    partner = at(0, 0, 1 - core)
    x_mates = [at(0, 0, which, d) for which in (core, 1 - core) for d in range(1, ROWS)]
    links = [at(dy, dz, core) for dy, dz in LINKS]

    loads = [
        pltpu.make_async_copy(basis_hbm, basis_ref, local_sem.at[0]),
        pltpu.make_async_copy(phase_hbm, phase_ref, local_sem.at[1]),
        pltpu.make_async_copy(receivers_ref, rx_ref.at[0, core], local_sem.at[2]),
        pltpu.make_async_copy(coupling_hbm, coupling_ref, local_sem.at[3]),
        pltpu.make_async_copy(order_hbm, order_ref, local_sem.at[4]),
        pltpu.make_async_copy(table_hbm, table_ref, local_sem.at[5]),
    ]
    for load in loads:
        load.start()
    barrier = pltpu.get_barrier_semaphore()
    greeted = [partner, *links, *x_mates]
    for device in greeted:
        pl.semaphore_signal(barrier, inc=1, device_id=device, device_id_type=MESH)
    pl.semaphore_wait(barrier, len(greeted))

    ones = [
        remote(
            sources_ref.at[half, :, tree // 4, :, pl.ds(128 * (tree % 4), 128)],
            taken_ref.at[half, tree],
            one_send.at[half * OWN + tree],
            one_recv.at[half * OWN + tree],
            links[tree],
        )
        for half in range(2)
        for tree in range(OWN)
    ]
    for copy in ones:
        copy.start()
    rx = []
    for n, (dx, flip) in enumerate((dx, flip) for flip in (0, 1) for dx in range(ROWS)):
        if n:
            rx.append(
                remote(
                    receivers_ref,
                    rx_ref.at[(ROWS - dx) % ROWS, core],
                    rx_send.at[n],
                    rx_recv.at[n],
                    at(0, 0, core if flip == 0 else 1 - core, dx),
                )
            )
    for copy in rx:
        copy.start()
    loads[3].wait()
    for c in range(8):
        gain_ref[core, c : c + 1, :] = jnp.full((1, 128), coupling_ref[c], jnp.float32)
    gains = remote(gain_ref.at[core], gain_ref.at[core], gain_sem.at[0], gain_sem.at[1], partner)
    gains.start()

    loads[0].wait()
    loads[1].wait()
    tables = lax.dot_general(
        basis_ref[...],
        phase_ref[...],
        (((1,), (0,)), ((), ())),
        precision=lax.Precision.HIGHEST,
        preferred_element_type=jnp.float32,
    )
    band = tables.shape[1] // 2
    cosine, sine = tables[:, :band], tables[:, band:]

    loads[2].wait()
    for copy in rx:
        copy.wait_recv()

    def project(n, carry):
        place, which = n // 2, n % 2
        turned = place % ROWS
        slab = jnp.where(turned == 2, 3, jnp.where(turned == 3, 2, turned))
        spectra = rx_ref[slab, which, place // ROWS].astype(jnp.float32)
        for c in range(8):
            real, imag = spectra[c : c + 1, :band], spectra[c : c + 1, band:]
            both = jnp.concatenate([real * cosine - imag * sine, real * sine + imag * cosine], axis=1)
            first = pl.multiple_of(which * 256 + c * 32, 32)
            rows_ref[place, pl.ds(first, 32), :] = both.astype(jnp.bfloat16)
        return carry

    lax.fori_loop(0, 2 * CHUNKS, project, 0)

    loads[4].wait()
    loads[5].wait()
    owners = [order_ref[b] for b in range(2)]
    roots = [(o // 2 % RING, o // (2 * RING), o % 2) for o in owners]
    relative = [((me_y - y + RING) % RING, (me_z - z + RING) % RING) for y, z, _ in roots]

    crossings = []
    for half in range(2):
        for tree in range(OWN):
            ones[half * OWN + tree].wait_recv()
        for b in range(2):
            kept = taken_ref[half, 0]
            for tree in range(1, OWN):
                dy, dz = LINKS[tree]
                here = jnp.logical_and(relative[b][0] == dy % RING, relative[b][1] == dz % RING)
                kept = jnp.where(here, taken_ref[half, tree], kept)
            pick_ref[half, b] = kept
        for n in range(1, 2 * ROWS):
            flip, dx = divmod(n, ROWS)
            which = core if flip == 0 else 1 - core
            place = half * ROWS + SLABS.index((ROWS - dx) % ROWS)
            crossings.append(
                remote(
                    pick_ref.at[half, which, (me_x + dx) % ROWS],
                    both_ref.at[core, place],
                    x_send.at[half * 2 * ROWS + n],
                    x_recv.at[half * 2 * ROWS + n],
                    at(0, 0, which, dx),
                )
            )
            crossings[-1].start()
        both_ref[core, half * ROWS] = pick_ref[half, core, me_x]
    mine = core == 0
    root_core = jnp.where(mine, roots[0][2], roots[1][2])

    rel_y = jnp.where(mine, relative[0][0], relative[1][0])
    rel_z = jnp.where(mine, relative[0][1], relative[1][1])
    entry = (rel_y * RING + rel_z) * 3 * OWN
    forward = [table_ref[entry + link] for link in range(OWN)]
    place_of = [table_ref[entry + OWN + tree] for tree in range(OWN)]
    level_of = [table_ref[entry + 2 * OWN + tree] for tree in range(OWN)]

    def landing(link, hop, lane):
        if isinstance(hop, int) and hop == HOPS:
            return came_refs[LAG + lane].at[link]
        return came_refs[lane].at[link * HOPS + hop]

    def flow(link, hop, lane, leaving=False):
        number = link * SLOTS + hop * LAG + lane
        return remote(
            send_ref.at[number],
            came_refs[0].at[0] if leaving else landing(link, hop, lane),
            flow_send.at[number],
            flow_recv.at[number],
            links[link],
        )

    def pass_on(hop, lane, own):
        heard = []
        if not (isinstance(hop, int) and hop == 0):
            for link in range(OWN):
                flow(link, hop - 1, lane).wait_recv()
            heard = [came_refs[lane][link * HOPS + hop - 1] for link in range(OWN)]
        for link in range(OWN):
            value = heard[0] if own is None else own
            for n, got in enumerate(heard):
                value = jnp.where(forward[link] == n, got, value)
            send_ref[link * SLOTS + hop * LAG + lane] = value
            flow(link, hop, lane).start()

    for slot in range(CHUNKS):
        half, place = divmod(slot, ROWS)
        dx = (ROWS - SLABS[place]) % ROWS
        for n in (dx, ROWS + dx):
            if n:
                crossings[half * (2 * ROWS - 1) + n - 1].wait_recv()
        own = jnp.where(root_core == 0, both_ref[0, slot], both_ref[1, slot])
        own_ref[slot] = own
        pass_on(slot // LAG, slot % LAG, own)
    for lane in range(CHUNKS - LAG, LAG):
        pass_on(1, lane, None)

    def later(hop, carry):
        for lane in range(LAG):
            pass_on(hop, lane, None)
        return carry

    lax.fori_loop(2, HOPS, later, 0)
    for lane in range(CHUNKS - LAG):
        pass_on(HOPS, lane, None)

    for chunk in range(CHUNKS):
        late, lane = divmod(chunk, LAG)
        for link in range(OWN):
            if late:
                flow(link, HOPS, lane).wait_recv()
            elif lane >= CHUNKS - LAG:
                flow(link, HOPS - 1, lane).wait_recv()
        halves = []
        for half in range(2):
            pieces = []
            for tree in range(4 * half, 4 * half + 4):
                if late:
                    last = level_of[tree] == HOPS
                    got = came_refs[lane][place_of[tree] + jnp.where(last, 0, 1)]
                    got = jnp.where(last, came_refs[LAG + lane][place_of[tree] // HOPS], got)
                else:
                    got = came_refs[lane][place_of[tree]]
                pieces.append(jnp.where(level_of[tree] == 0, own_ref[chunk], got))
            halves.append(jnp.concatenate(pieces, axis=1))
        product = lax.dot_general(
            rows_ref[chunk],
            jnp.concatenate(halves, axis=0),
            (((1,), (1,)), ((), ())),
            preferred_element_type=jnp.float32,
        )
        product = product.reshape(16, 32, 64)
        if chunk == 0:
            result_ref[...] = product
        else:
            result_ref[...] += product
    gains.wait()
    power = jnp.zeros((32, 64), jnp.float32)
    for c in range(16):
        piece = result_ref[c] * gain_ref[c // 8, c % 8 : c % 8 + 1, :64]
        result_ref[c] = piece
        power = power + piece * piece
    power = jnp.sum(power, axis=0, keepdims=True)
    part_ref[...] = jnp.concatenate([power, power], axis=1)

    def total(n):
        return remote(
            part_ref,
            plane_ref.at[pl.ds(n, 1)],
            plane_send.at[n],
            plane_recv.at[n],
            at(n // RING, n % RING, core),
        )

    def start(n, carry):
        total(n).start()
        return carry

    lax.fori_loop(1, RING * RING, start, 0)
    plane_ref[0:1, :] = part_ref[...]
    other = remote(
        result_ref.at[pl.ds((1 - core) * 8, 8)],
        other_ref,
        other_sem.at[0],
        other_sem.at[1],
        partner,
    )
    other.start()

    for copy in [*ones, *rx, *crossings]:
        copy.wait_send()

    def left(slot, carry):
        for link in range(OWN):
            flow(link, 0, slot, True).wait_send()
        return carry

    lax.fori_loop(0, SLOTS, left, 0)
    other.wait()

    def arrived(n, carry):
        total(n).wait()
        return carry

    lax.fori_loop(1, RING * RING, arrived, 0)
    sum_ref[...] = jnp.sum(plane_ref[...], axis=0, keepdims=True)
    mate = remote(sum_ref, mate_ref, mate_sem.at[0], mate_sem.at[1], partner)
    mate.start()

    def scale(ref):
        return lax.rsqrt(ref[:, :64] / 32768.0 + 1e-05)

    out_ref[core] = result_ref[pl.ds(core * 8, 8)] * scale(sum_ref)
    mate.wait()
    out_ref[1 - core] = other_ref[...] * scale(mate_ref)


def put_out(result_ref, out_ref, sem):
    copy = pltpu.make_async_copy(result_ref, out_ref, sem)
    copy.start()
    copy.wait()


def per_device(receivers, sources, coupling, lag_basis, source_order):
    lags, basis_count = lag_basis.shape
    bf16, f32 = jnp.bfloat16, jnp.float32
    dma = pltpu.SemaphoreType.DMA
    anywhere = pl.BlockSpec(memory_space=pl.ANY)
    result = pl.pallas_call(
        kernel,
        out_shape=pltpu.VMEM((2, 8, 32, 64), f32),
        in_specs=[anywhere] * 7,
        out_specs=pl.BlockSpec(memory_space=pltpu.VMEM),
        scratch_shapes=[
            pltpu.SMEM(coupling.shape, f32),
            pltpu.SMEM(source_order.shape, jnp.int32),
            pltpu.SMEM((RING * RING * 3 * OWN,), jnp.int32),
            pltpu.VMEM((basis_count, lags), f32),
            pltpu.VMEM((lags, 512), f32),
            pltpu.VMEM((ROWS, 2, 2, 8, 512), bf16),
            pltpu.VMEM((2, 8, 128), f32),
            pltpu.VMEM((2, OWN, *PIECE), bf16),
            pltpu.VMEM((2, 2, *PIECE), bf16),
            pltpu.VMEM((2, CHUNKS, 32, 128), bf16),
            pltpu.VMEM((CHUNKS, 32, 128), bf16),
            pltpu.VMEM((OWN * SLOTS, 32, 128), bf16),
            pltpu.VMEM((CHUNKS, 512, 512), bf16),
            pltpu.VMEM((16, 32, 64), f32),
            pltpu.VMEM((8, 32, 64), f32),
            pltpu.VMEM((1, 128), f32),
            pltpu.VMEM((RING * RING, 128), f32),
            pltpu.VMEM((1, 128), f32),
            pltpu.VMEM((1, 128), f32),
            dma((6,)),
            dma((2 * ROWS,)),
            dma((2 * ROWS,)),
            dma((2,)),
            dma((2 * OWN,)),
            dma((2 * OWN,)),
            dma((4 * ROWS,)),
            dma((4 * ROWS,)),
            dma((OWN * SLOTS,)),
            dma((OWN * SLOTS,)),
            dma((2,)),
            dma((RING * RING,)),
            dma((RING * RING,)),
            dma((2,)),
            *[pltpu.VMEM((OWN * HOPS, 32, 128), bf16)] * LAG,
            *[pltpu.VMEM((OWN, 32, 128), bf16)] * (CHUNKS - LAG),
        ],
        compiler_params=pltpu.CompilerParams(collective_id=0, has_side_effects=True),
    )(
        receivers,
        sources.reshape(2, ROWS, 2, 32, 512),
        lag_basis.T,
        jnp.asarray(phase_table(256, lags)),
        coupling,
        source_order,
        jnp.asarray(tree_tables()),
    )
    return pl.pallas_call(
        put_out,
        out_shape=jax.ShapeDtypeStruct(result.shape, f32),
        in_specs=[pl.BlockSpec(memory_space=pltpu.VMEM)],
        out_specs=anywhere,
        scratch_shapes=[dma],
        compiler_params=pltpu.CompilerParams(vmem_limit_bytes=1 << 20),
    )(result)


def solution(mesh):
    return jax.shard_map(
        per_device,
        mesh=mesh,
        in_specs=(P("win", "chan", None), P("win", "chan", None), P("chan"), P(), P()),
        out_specs=P(None, "chan", None, "win"),
        check_vma=False,
    )
```

```python
import functools
import math

import jax
import jax.numpy as jnp
import numpy as np
from jax import lax
from jax.experimental import pallas as pl
from jax.experimental.pallas import tpu as pltpu
from jax.sharding import PartitionSpec as P

MESH = pl.DeviceIdType.MESH
RING = 8
ROWS = 4
TURNS = ((1, 0), (0, 1), (-1, 0), (0, -1))
LINKS = TURNS + tuple((2 * y, 2 * z) for y, z in TURNS)
TREES = (
    (
        (2, 6, 2, 2, 2, 2, 2, 2),
        (-1, 1, 5, 5, 5, 7, 7, 3),
        (0, 1, 4, 2, 2, 2, 0, 7),
        (4, 3, 5, 4, 5, 4, 4, 5),
        (0, 3, 0, 0, 0, 0, 0, 2),
        (4, 5, 4, 4, 4, 4, 4, 3),
        (0, 2, 0, 2, 2, 6, 0, 2),
        (3, 6, 7, 6, 6, 5, 5, 6),
    ),
    (
        (6, 1, 6, 6, 6, 6, 7, 6),
        (2, 3, 2, 2, 1, 6, 6, 6),
        (-1, 3, 5, 1, 5, 7, 3, 3),
        (0, 2, 0, 0, 7, 0, 2, 0),
        (4, 1, 4, 5, 7, 3, 7, 5),
        (0, 0, 1, 0, 0, 0, 0, 4),
        (4, 0, 4, 4, 4, 4, 4, 0),
        (6, 3, 6, 1, 5, 2, 4, 4),
    ),
)
HOPS = 4
CHUNKS = 2 * ROWS
LAG = 6
SLOTS = CHUNKS + (HOPS - 1) * LAG
OWN = len(LINKS)
LONG_FIRST = (4, 5, 6, 7, 0, 1, 2, 3)
FAR_FIRST = sorted(
    range(1, RING * RING),
    key=lambda n: -sum(min(d, RING - d) for d in divmod(n, RING)),
)
PIECE = (ROWS, 32, 128)
SLABS = (0, 1, 3, 2)


def turn(node, times):
    for _ in range(times % 4):
        node = ((-node[1]) % RING, node[0])
    return node


def step_from(node, link, sign=1):
    return tuple((node[i] + sign * LINKS[link][i]) % RING for i in range(2))


def tree_tables():
    def reached(tree, node):
        y, z = turn(node, -tree)
        link = TREES[tree // 4][y][z]
        return -1 if link < 0 else link // 4 * 4 + (link + tree) % 4

    def depth(tree, node):
        count = 0
        while (link := reached(tree, node)) >= 0:
            node = step_from(node, link, -1)
            count += 1
        return count

    table = np.zeros((RING * RING, 3 * OWN), np.int32)
    for y in range(RING):
        for z in range(RING):
            row = table[y * RING + z]
            for tree in range(OWN):
                link, level = reached(tree, (y, z)), depth(tree, (y, z))
                assert level <= HOPS
                row[OWN + tree] = 0 if level == 0 else link * HOPS + level - 1
                row[2 * OWN + tree] = level
                for out in range(OWN):
                    if reached(tree, step_from((y, z), out)) == out:
                        row[out] = OWN if level == 0 else link
    return table.reshape(-1)


def phase_table(band, lags):
    turns = np.arange(lags)[:, None] - lags // 2
    phase = (turns * np.arange(band)[None, :]) % (2 * band) * (math.pi / band)
    return np.concatenate([np.cos(phase), np.sin(phase)], axis=1).astype(np.float32)


def kernel(
    receivers_ref,
    sources_ref,
    basis_hbm,
    phase_hbm,
    coupling_hbm,
    order_hbm,
    table_hbm,
    out_ref,
    coupling_ref,
    order_ref,
    table_ref,
    basis_ref,
    phase_ref,
    rx_ref,
    gain_ref,
    taken_ref,
    pick_ref,
    both_ref,
    own_ref,
    send_ref,
    rows_ref,
    result_ref,
    other_ref,
    part_ref,
    plane_ref,
    sum_ref,
    mate_ref,
    local_sem,
    rx_send,
    rx_recv,
    gain_sem,
    one_send,
    one_recv,
    x_send,
    x_recv,
    flow_send,
    flow_recv,
    other_sem,
    plane_send,
    plane_recv,
    mate_sem,
    *came_refs,
):
    chan, me_x = lax.axis_index("chan"), lax.axis_index("win")
    core = chan % 2
    me_y = chan // 2 % RING
    me_z = chan // (2 * RING)

    def at(dy, dz, which, dx=0):
        y, z = (me_y + dy) % RING, (me_z + dz) % RING
        return ((z * RING + y) * 2 + which, (me_x + dx) % ROWS)

    def remote(src, dst, send, recv, device):
        return pltpu.make_async_remote_copy(
            src_ref=src, dst_ref=dst, send_sem=send, recv_sem=recv, device_id=device, device_id_type=MESH
        )

    partner = at(0, 0, 1 - core)
    x_mates = [at(0, 0, which, d) for which in (core, 1 - core) for d in range(1, ROWS)]
    links = [at(dy, dz, core) for dy, dz in LINKS]

    loads = [
        pltpu.make_async_copy(basis_hbm, basis_ref, local_sem.at[0]),
        pltpu.make_async_copy(phase_hbm, phase_ref, local_sem.at[1]),
        pltpu.make_async_copy(receivers_ref, rx_ref.at[0, core], local_sem.at[2]),
        pltpu.make_async_copy(coupling_hbm, coupling_ref, local_sem.at[3]),
        pltpu.make_async_copy(order_hbm, order_ref, local_sem.at[4]),
        pltpu.make_async_copy(table_hbm, table_ref, local_sem.at[5]),
    ]
    for load in loads:
        load.start()
    barrier = pltpu.get_barrier_semaphore()
    greeted = [partner, *links, *x_mates]
    for device in greeted:
        pl.semaphore_signal(barrier, inc=1, device_id=device, device_id_type=MESH)
    pl.semaphore_wait(barrier, len(greeted))

    ones = [
        remote(
            sources_ref.at[half, :, tree // 4, :, pl.ds(128 * (tree % 4), 128)],
            taken_ref.at[half, tree],
            one_send.at[half * OWN + tree],
            one_recv.at[half * OWN + tree],
            links[tree],
        )
        for half in range(2)
        for tree in range(OWN)
    ]
    for half in range(2):
        for tree in LONG_FIRST:
            ones[half * OWN + tree].start()
    rx = []
    for n, (dx, flip) in enumerate((dx, flip) for flip in (0, 1) for dx in range(ROWS)):
        if n:
            rx.append(
                remote(
                    receivers_ref,
                    rx_ref.at[(ROWS - dx) % ROWS, core],
                    rx_send.at[n],
                    rx_recv.at[n],
                    at(0, 0, core if flip == 0 else 1 - core, dx),
                )
            )
    for copy in rx:
        copy.start()
    loads[3].wait()
    for c in range(8):
        gain_ref[core, c : c + 1, :] = jnp.full((1, 128), coupling_ref[c], jnp.float32)
    gains = remote(gain_ref.at[core], gain_ref.at[core], gain_sem.at[0], gain_sem.at[1], partner)
    gains.start()

    loads[0].wait()
    loads[1].wait()
    tables = lax.dot_general(
        basis_ref[...],
        phase_ref[...],
        (((1,), (0,)), ((), ())),
        precision=lax.Precision.HIGHEST,
        preferred_element_type=jnp.float32,
    )
    band = tables.shape[1] // 2
    cosine, sine = tables[:, :band], tables[:, band:]

    loads[2].wait()
    for copy in rx:
        copy.wait_recv()

    def project(n, carry):
        place, which = n // 2, n % 2
        turned = place % ROWS
        slab = jnp.where(turned == 2, 3, jnp.where(turned == 3, 2, turned))
        spectra = rx_ref[slab, which, place // ROWS].astype(jnp.float32)
        for c in range(8):
            real, imag = spectra[c : c + 1, :band], spectra[c : c + 1, band:]
            both = jnp.concatenate([real * cosine - imag * sine, real * sine + imag * cosine], axis=1)
            first = pl.multiple_of(which * 256 + c * 32, 32)
            rows_ref[place, pl.ds(first, 32), :] = both.astype(jnp.bfloat16)
        return carry

    lax.fori_loop(0, 2 * CHUNKS, project, 0)

    loads[4].wait()
    loads[5].wait()
    owners = [order_ref[b] for b in range(2)]
    roots = [(o // 2 % RING, o // (2 * RING), o % 2) for o in owners]
    relative = [((me_y - y + RING) % RING, (me_z - z + RING) % RING) for y, z, _ in roots]

    crossings = []
    for half in range(2):
        for tree in range(OWN):
            ones[half * OWN + tree].wait_recv()
        for b in range(2):
            kept = taken_ref[half, 0]
            for tree in range(1, OWN):
                dy, dz = LINKS[tree]
                here = jnp.logical_and(relative[b][0] == dy % RING, relative[b][1] == dz % RING)
                kept = jnp.where(here, taken_ref[half, tree], kept)
            pick_ref[half, b] = kept
        for n in range(1, 2 * ROWS):
            flip, dx = divmod(n, ROWS)
            which = core if flip == 0 else 1 - core
            place = half * ROWS + SLABS.index((ROWS - dx) % ROWS)
            crossings.append(
                remote(
                    pick_ref.at[half, which, (me_x + dx) % ROWS],
                    both_ref.at[core, place],
                    x_send.at[half * 2 * ROWS + n],
                    x_recv.at[half * 2 * ROWS + n],
                    at(0, 0, which, dx),
                )
            )
        for n in (2, ROWS + 2, 1, 3, ROWS + 1, ROWS + 3, ROWS):
            crossings[half * (2 * ROWS - 1) + n - 1].start()
        both_ref[core, half * ROWS] = pick_ref[half, core, me_x]
    mine = core == 0
    root_core = jnp.where(mine, roots[0][2], roots[1][2])

    rel_y = jnp.where(mine, relative[0][0], relative[1][0])
    rel_z = jnp.where(mine, relative[0][1], relative[1][1])
    entry = (rel_y * RING + rel_z) * 3 * OWN
    forward = [table_ref[entry + link] for link in range(OWN)]
    place_of = [table_ref[entry + OWN + tree] for tree in range(OWN)]
    level_of = [table_ref[entry + 2 * OWN + tree] for tree in range(OWN)]

    def landing(link, hop, lane):
        if isinstance(hop, int) and hop == HOPS:
            return came_refs[LAG + lane].at[link]
        return came_refs[lane].at[link * HOPS + hop]

    def flow(link, hop, lane, leaving=False):
        number = link * SLOTS + hop * LAG + lane
        return remote(
            send_ref.at[number],
            came_refs[0].at[0] if leaving else landing(link, hop, lane),
            flow_send.at[number],
            flow_recv.at[number],
            links[link],
        )

    def pass_on(hop, lane, own):
        heard = []
        if not (isinstance(hop, int) and hop == 0):
            for link in range(OWN):
                flow(link, hop - 1, lane).wait_recv()
            heard = [came_refs[lane][link * HOPS + hop - 1] for link in range(OWN)]
        for link in LONG_FIRST:
            value = heard[0] if own is None else own
            for n, got in enumerate(heard):
                value = jnp.where(forward[link] == n, got, value)
            send_ref[link * SLOTS + hop * LAG + lane] = value
            flow(link, hop, lane).start()

    for slot in range(CHUNKS):
        half, place = divmod(slot, ROWS)
        dx = (ROWS - SLABS[place]) % ROWS
        for n in (dx, ROWS + dx):
            if n:
                crossings[half * (2 * ROWS - 1) + n - 1].wait_recv()
        own = jnp.where(root_core == 0, both_ref[0, slot], both_ref[1, slot])
        own_ref[slot] = own
        pass_on(slot // LAG, slot % LAG, own)
    for lane in range(CHUNKS - LAG, LAG):
        pass_on(1, lane, None)

    def later(hop, carry):
        for lane in range(LAG):
            pass_on(hop, lane, None)
        return carry

    lax.fori_loop(2, HOPS, later, 0)
    for lane in range(CHUNKS - LAG):
        pass_on(HOPS, lane, None)

    for chunk in range(CHUNKS):
        late, lane = divmod(chunk, LAG)
        for link in range(OWN):
            if late:
                flow(link, HOPS, lane).wait_recv()
            elif lane >= CHUNKS - LAG:
                flow(link, HOPS - 1, lane).wait_recv()
        halves = []
        for half in range(2):
            pieces = []
            for tree in range(4 * half, 4 * half + 4):
                if late:
                    last = level_of[tree] == HOPS
                    got = came_refs[lane][place_of[tree] + jnp.where(last, 0, 1)]
                    got = jnp.where(last, came_refs[LAG + lane][place_of[tree] // HOPS], got)
                else:
                    got = came_refs[lane][place_of[tree]]
                pieces.append(jnp.where(level_of[tree] == 0, own_ref[chunk], got))
            halves.append(jnp.concatenate(pieces, axis=1))
        product = lax.dot_general(
            rows_ref[chunk],
            jnp.concatenate(halves, axis=0),
            (((1,), (1,)), ((), ())),
            preferred_element_type=jnp.float32,
        )
        product = product.reshape(16, 32, 64)
        if chunk == 0:
            result_ref[...] = product
        else:
            result_ref[...] += product
    gains.wait()
    power = jnp.zeros((32, 64), jnp.float32)
    for c in range(16):
        piece = result_ref[c] * gain_ref[c // 8, c % 8 : c % 8 + 1, :64]
        result_ref[c] = piece
        power = power + piece * piece
    power = jnp.sum(power, axis=0, keepdims=True)
    part_ref[...] = jnp.concatenate([power, power], axis=1)

    def total(n):
        return remote(
            part_ref,
            plane_ref.at[pl.ds(n, 1)],
            plane_send.at[n],
            plane_recv.at[n],
            at(n // RING, n % RING, core),
        )

    for n in FAR_FIRST:
        total(n).start()
    plane_ref[0:1, :] = part_ref[...]
    other = remote(
        result_ref.at[pl.ds((1 - core) * 8, 8)],
        other_ref,
        other_sem.at[0],
        other_sem.at[1],
        partner,
    )
    other.start()

    for copy in [*ones, *rx, *crossings]:
        copy.wait_send()

    def left(slot, carry):
        for link in range(OWN):
            flow(link, 0, slot, True).wait_send()
        return carry

    lax.fori_loop(0, SLOTS, left, 0)
    other.wait()

    def arrived(n, carry):
        total(n).wait()
        return carry

    lax.fori_loop(1, RING * RING, arrived, 0)
    sum_ref[...] = jnp.sum(plane_ref[...], axis=0, keepdims=True)
    mate = remote(sum_ref, mate_ref, mate_sem.at[0], mate_sem.at[1], partner)
    mate.start()

    def scale(ref):
        return lax.rsqrt(ref[:, :64] / 32768.0 + 1e-05)

    out_ref[core] = result_ref[pl.ds(core * 8, 8)] * scale(sum_ref)
    mate.wait()
    out_ref[1 - core] = other_ref[...] * scale(mate_ref)


def put_out(result_ref, out_ref, sem):
    copy = pltpu.make_async_copy(result_ref, out_ref, sem)
    copy.start()
    copy.wait()


def per_device(receivers, sources, coupling, lag_basis, source_order):
    lags, basis_count = lag_basis.shape
    bf16, f32 = jnp.bfloat16, jnp.float32
    dma = pltpu.SemaphoreType.DMA
    anywhere = pl.BlockSpec(memory_space=pl.ANY)
    result = pl.pallas_call(
        kernel,
        out_shape=pltpu.VMEM((2, 8, 32, 64), f32),
        in_specs=[anywhere] * 7,
        out_specs=pl.BlockSpec(memory_space=pltpu.VMEM),
        scratch_shapes=[
            pltpu.SMEM(coupling.shape, f32),
            pltpu.SMEM(source_order.shape, jnp.int32),
            pltpu.SMEM((RING * RING * 3 * OWN,), jnp.int32),
            pltpu.VMEM((basis_count, lags), f32),
            pltpu.VMEM((lags, 512), f32),
            pltpu.VMEM((ROWS, 2, 2, 8, 512), bf16),
            pltpu.VMEM((2, 8, 128), f32),
            pltpu.VMEM((2, OWN, *PIECE), bf16),
            pltpu.VMEM((2, 2, *PIECE), bf16),
            pltpu.VMEM((2, CHUNKS, 32, 128), bf16),
            pltpu.VMEM((CHUNKS, 32, 128), bf16),
            pltpu.VMEM((OWN * SLOTS, 32, 128), bf16),
            pltpu.VMEM((CHUNKS, 512, 512), bf16),
            pltpu.VMEM((16, 32, 64), f32),
            pltpu.VMEM((8, 32, 64), f32),
            pltpu.VMEM((1, 128), f32),
            pltpu.VMEM((RING * RING, 128), f32),
            pltpu.VMEM((1, 128), f32),
            pltpu.VMEM((1, 128), f32),
            dma((6,)),
            dma((2 * ROWS,)),
            dma((2 * ROWS,)),
            dma((2,)),
            dma((2 * OWN,)),
            dma((2 * OWN,)),
            dma((4 * ROWS,)),
            dma((4 * ROWS,)),
            dma((OWN * SLOTS,)),
            dma((OWN * SLOTS,)),
            dma((2,)),
            dma((RING * RING,)),
            dma((RING * RING,)),
            dma((2,)),
            *[pltpu.VMEM((OWN * HOPS, 32, 128), bf16)] * LAG,
            *[pltpu.VMEM((OWN, 32, 128), bf16)] * (CHUNKS - LAG),
        ],
        compiler_params=pltpu.CompilerParams(collective_id=0, has_side_effects=True),
    )(
        receivers,
        sources.reshape(2, ROWS, 2, 32, 512),
        lag_basis.T,
        jnp.asarray(phase_table(256, lags)),
        coupling,
        source_order,
        jnp.asarray(tree_tables()),
    )
    return pl.pallas_call(
        put_out,
        out_shape=jax.ShapeDtypeStruct(result.shape, f32),
        in_specs=[pl.BlockSpec(memory_space=pltpu.VMEM)],
        out_specs=anywhere,
        scratch_shapes=[dma],
        compiler_params=pltpu.CompilerParams(vmem_limit_bytes=1 << 20),
    )(result)


def solution(mesh):
    return jax.shard_map(
        per_device,
        mesh=mesh,
        in_specs=(P("win", "chan", None), P("win", "chan", None), P("chan"), P(), P()),
        out_specs=P(None, "chan", None, "win"),
        check_vma=False,
    )
```

```python
import functools
import math

import jax
import jax.numpy as jnp
import numpy as np
from jax import lax
from jax.experimental import pallas as pl
from jax.experimental.pallas import tpu as pltpu
from jax.sharding import PartitionSpec as P

MESH = pl.DeviceIdType.MESH
RING = 8
ROWS = 4
TURNS = ((1, 0), (0, 1), (-1, 0), (0, -1))
LINKS = TURNS + tuple((2 * y, 2 * z) for y, z in TURNS)
TREES = (
    (
        (2, 6, 2, 2, 2, 2, 2, 2),
        (-1, 1, 5, 5, 5, 7, 7, 3),
        (0, 1, 4, 2, 2, 2, 0, 7),
        (4, 3, 5, 4, 5, 4, 4, 5),
        (0, 3, 0, 0, 0, 0, 0, 2),
        (4, 5, 4, 4, 4, 4, 4, 3),
        (0, 2, 0, 2, 2, 6, 0, 2),
        (3, 6, 7, 6, 6, 5, 5, 6),
    ),
    (
        (6, 1, 6, 6, 6, 6, 7, 6),
        (2, 3, 2, 2, 1, 6, 6, 6),
        (-1, 3, 5, 1, 5, 7, 3, 3),
        (0, 2, 0, 0, 7, 0, 2, 0),
        (4, 1, 4, 5, 7, 3, 7, 5),
        (0, 0, 1, 0, 0, 0, 0, 4),
        (4, 0, 4, 4, 4, 4, 4, 0),
        (6, 3, 6, 1, 5, 2, 4, 4),
    ),
)
HOPS = 4
CHUNKS = 2 * ROWS
LAG = 6
SLOTS = CHUNKS + (HOPS - 1) * LAG
OWN = len(LINKS)
LONG_FIRST = (4, 5, 6, 7, 0, 1, 2, 3)
FAR_FIRST = sorted(
    range(1, RING * RING),
    key=lambda n: -sum(min(d, RING - d) for d in divmod(n, RING)),
)
PIECE = (ROWS, 32, 128)
WINDOWS = ((0, 0), (0, 1), (1, 0), (3, 0), (2, 0), (1, 1), (3, 1), (2, 1))


def turn(node, times):
    for _ in range(times % 4):
        node = ((-node[1]) % RING, node[0])
    return node


def step_from(node, link, sign=1):
    return tuple((node[i] + sign * LINKS[link][i]) % RING for i in range(2))


def tree_tables():
    def reached(tree, node):
        y, z = turn(node, -tree)
        link = TREES[tree // 4][y][z]
        return -1 if link < 0 else link // 4 * 4 + (link + tree) % 4

    def depth(tree, node):
        count = 0
        while (link := reached(tree, node)) >= 0:
            node = step_from(node, link, -1)
            count += 1
        return count

    table = np.zeros((RING * RING, 3 * OWN), np.int32)
    for y in range(RING):
        for z in range(RING):
            row = table[y * RING + z]
            for tree in range(OWN):
                link, level = reached(tree, (y, z)), depth(tree, (y, z))
                assert level <= HOPS
                row[OWN + tree] = 0 if level == 0 else link * HOPS + level - 1
                row[2 * OWN + tree] = level
                for out in range(OWN):
                    if reached(tree, step_from((y, z), out)) == out:
                        row[out] = OWN if level == 0 else link
    return table.reshape(-1)


def phase_table(band, lags):
    turns = np.arange(lags)[:, None] - lags // 2
    phase = (turns * np.arange(band)[None, :]) % (2 * band) * (math.pi / band)
    return np.concatenate([np.cos(phase), np.sin(phase)], axis=1).astype(np.float32)


def kernel(
    receivers_ref,
    sources_ref,
    basis_hbm,
    phase_hbm,
    coupling_hbm,
    order_hbm,
    table_hbm,
    out_ref,
    coupling_ref,
    order_ref,
    table_ref,
    basis_ref,
    phase_ref,
    rx_ref,
    gain_ref,
    taken_ref,
    pick_ref,
    both_ref,
    own_ref,
    send_ref,
    rows_ref,
    result_ref,
    other_ref,
    part_ref,
    plane_ref,
    sum_ref,
    mate_ref,
    local_sem,
    rx_send,
    rx_recv,
    gain_sem,
    one_send,
    one_recv,
    x_send,
    x_recv,
    flow_send,
    flow_recv,
    other_sem,
    plane_send,
    plane_recv,
    mate_sem,
    *came_refs,
):
    chan, me_x = lax.axis_index("chan"), lax.axis_index("win")
    core = chan % 2
    me_y = chan // 2 % RING
    me_z = chan // (2 * RING)

    def at(dy, dz, which, dx=0):
        y, z = (me_y + dy) % RING, (me_z + dz) % RING
        return ((z * RING + y) * 2 + which, (me_x + dx) % ROWS)

    def remote(src, dst, send, recv, device):
        return pltpu.make_async_remote_copy(
            src_ref=src, dst_ref=dst, send_sem=send, recv_sem=recv, device_id=device, device_id_type=MESH
        )

    partner = at(0, 0, 1 - core)
    x_mates = [at(0, 0, which, d) for which in (core, 1 - core) for d in range(1, ROWS)]
    links = [at(dy, dz, core) for dy, dz in LINKS]

    loads = [
        pltpu.make_async_copy(basis_hbm, basis_ref, local_sem.at[0]),
        pltpu.make_async_copy(phase_hbm, phase_ref, local_sem.at[1]),
        pltpu.make_async_copy(receivers_ref, rx_ref.at[0, core], local_sem.at[2]),
        pltpu.make_async_copy(coupling_hbm, coupling_ref, local_sem.at[3]),
        pltpu.make_async_copy(order_hbm, order_ref, local_sem.at[4]),
        pltpu.make_async_copy(table_hbm, table_ref, local_sem.at[5]),
    ]
    barrier = pltpu.get_barrier_semaphore()
    greeted = [partner, *links, *x_mates]
    for device in greeted:
        pl.semaphore_signal(barrier, inc=1, device_id=device, device_id_type=MESH)
    for load in loads:
        load.start()
    pl.semaphore_wait(barrier, len(greeted))

    ones = [
        remote(
            sources_ref.at[half, :, tree // 4, :, pl.ds(128 * (tree % 4), 128)],
            taken_ref.at[half, tree],
            one_send.at[half * OWN + tree],
            one_recv.at[half * OWN + tree],
            links[tree],
        )
        for half in range(2)
        for tree in range(OWN)
    ]
    for half in range(2):
        for tree in LONG_FIRST:
            ones[half * OWN + tree].start()
    rx = []
    for n, (dx, flip) in enumerate((dx, flip) for flip in (0, 1) for dx in range(ROWS)):
        if n:
            rx.append(
                remote(
                    receivers_ref,
                    rx_ref.at[(ROWS - dx) % ROWS, core],
                    rx_send.at[n],
                    rx_recv.at[n],
                    at(0, 0, core if flip == 0 else 1 - core, dx),
                )
            )
    for copy in rx:
        copy.start()
    loads[3].wait()
    for c in range(8):
        gain_ref[core, c : c + 1, :] = jnp.full((1, 128), coupling_ref[c], jnp.float32)
    gains = remote(gain_ref.at[core], gain_ref.at[core], gain_sem.at[0], gain_sem.at[1], partner)
    gains.start()

    loads[0].wait()
    loads[1].wait()
    tables = lax.dot_general(
        basis_ref[...],
        phase_ref[...],
        (((1,), (0,)), ((), ())),
        precision=lax.Precision.HIGHEST,
        preferred_element_type=jnp.float32,
    )
    band = tables.shape[1] // 2
    cosine, sine = tables[:, :band], tables[:, band:]

    loads[2].wait()
    for copy in rx:
        copy.wait_recv()

    def project(n, carry):
        slab, half, which = n // 4, n // 2 % 2, n % 2
        place = jnp.where(slab == 1, 2, jnp.where(slab == 2, 4, 3)) + 3 * half
        place = jnp.where(slab == 0, half, place)
        spectra = rx_ref[slab, which, half].astype(jnp.float32)
        for c in range(8):
            real, imag = spectra[c : c + 1, :band], spectra[c : c + 1, band:]
            both = jnp.concatenate([real * cosine - imag * sine, real * sine + imag * cosine], axis=1)
            first = pl.multiple_of(which * 256 + c * 32, 32)
            rows_ref[place, pl.ds(first, 32), :] = both.astype(jnp.bfloat16)
        return carry

    lax.fori_loop(0, 2 * CHUNKS, project, 0)

    loads[4].wait()
    loads[5].wait()
    owners = [order_ref[b] for b in range(2)]
    roots = [(o // 2 % RING, o // (2 * RING), o % 2) for o in owners]
    relative = [((me_y - y + RING) % RING, (me_z - z + RING) % RING) for y, z, _ in roots]

    crossings = []
    for half in range(2):
        for tree in range(OWN):
            ones[half * OWN + tree].wait_recv()
        for b in range(2):
            kept = taken_ref[half, 0]
            for tree in range(1, OWN):
                dy, dz = LINKS[tree]
                here = jnp.logical_and(relative[b][0] == dy % RING, relative[b][1] == dz % RING)
                kept = jnp.where(here, taken_ref[half, tree], kept)
            pick_ref[half, b] = kept
        for n in range(1, 2 * ROWS):
            flip, dx = divmod(n, ROWS)
            which = core if flip == 0 else 1 - core
            place = WINDOWS.index(((ROWS - dx) % ROWS, half))
            crossings.append(
                remote(
                    pick_ref.at[half, which, (me_x + dx) % ROWS],
                    both_ref.at[core, place],
                    x_send.at[half * 2 * ROWS + n],
                    x_recv.at[half * 2 * ROWS + n],
                    at(0, 0, which, dx),
                )
            )
        for n in (2, ROWS + 2, 1, 3, ROWS + 1, ROWS + 3, ROWS):
            crossings[half * (2 * ROWS - 1) + n - 1].start()
        both_ref[core, half] = pick_ref[half, core, me_x]
    mine = core == 0
    root_core = jnp.where(mine, roots[0][2], roots[1][2])

    rel_y = jnp.where(mine, relative[0][0], relative[1][0])
    rel_z = jnp.where(mine, relative[0][1], relative[1][1])
    entry = (rel_y * RING + rel_z) * 3 * OWN
    forward = [table_ref[entry + link] for link in range(OWN)]
    place_of = [table_ref[entry + OWN + tree] for tree in range(OWN)]
    level_of = [table_ref[entry + 2 * OWN + tree] for tree in range(OWN)]

    def landing(link, hop, lane):
        if isinstance(hop, int) and hop == HOPS:
            return came_refs[LAG + lane].at[link]
        return came_refs[lane].at[link * HOPS + hop]

    def flow(link, hop, lane, leaving=False):
        number = link * SLOTS + hop * LAG + lane
        return remote(
            send_ref.at[number],
            came_refs[0].at[0] if leaving else landing(link, hop, lane),
            flow_send.at[number],
            flow_recv.at[number],
            links[link],
        )

    def pass_on(hop, lane, own):
        heard = []
        if not (isinstance(hop, int) and hop == 0):
            for link in range(OWN):
                flow(link, hop - 1, lane).wait_recv()
            heard = [came_refs[lane][link * HOPS + hop - 1] for link in range(OWN)]
        for link in LONG_FIRST:
            value = heard[0] if own is None else own
            for n, got in enumerate(heard):
                value = jnp.where(forward[link] == n, got, value)
            send_ref[link * SLOTS + hop * LAG + lane] = value
            flow(link, hop, lane).start()

    for slot in range(CHUNKS):
        slab, half = WINDOWS[slot]
        dx = (ROWS - slab) % ROWS
        for n in (dx, ROWS + dx):
            if n:
                crossings[half * (2 * ROWS - 1) + n - 1].wait_recv()
        own = jnp.where(root_core == 0, both_ref[0, slot], both_ref[1, slot])
        own_ref[slot] = own
        pass_on(slot // LAG, slot % LAG, own)
    for lane in range(CHUNKS - LAG, LAG):
        pass_on(1, lane, None)

    def later(hop, carry):
        for lane in range(LAG):
            pass_on(hop, lane, None)
        return carry

    lax.fori_loop(2, HOPS, later, 0)
    for lane in range(CHUNKS - LAG):
        pass_on(HOPS, lane, None)

    for chunk in range(CHUNKS):
        late, lane = divmod(chunk, LAG)
        for link in range(OWN):
            if late:
                flow(link, HOPS, lane).wait_recv()
            elif lane >= CHUNKS - LAG:
                flow(link, HOPS - 1, lane).wait_recv()
        halves = []
        for half in range(2):
            pieces = []
            for tree in range(4 * half, 4 * half + 4):
                if late:
                    last = level_of[tree] == HOPS
                    got = came_refs[lane][place_of[tree] + jnp.where(last, 0, 1)]
                    got = jnp.where(last, came_refs[LAG + lane][place_of[tree] // HOPS], got)
                else:
                    got = came_refs[lane][place_of[tree]]
                pieces.append(jnp.where(level_of[tree] == 0, own_ref[chunk], got))
            halves.append(jnp.concatenate(pieces, axis=1))
        product = lax.dot_general(
            rows_ref[chunk],
            jnp.concatenate(halves, axis=0),
            (((1,), (1,)), ((), ())),
            preferred_element_type=jnp.float32,
        )
        product = product.reshape(16, 32, 64)
        if chunk == 0:
            result_ref[...] = product
        elif chunk < CHUNKS - 1:
            result_ref[...] += product
    gains.wait()
    power = jnp.zeros((32, 64), jnp.float32)
    for c in range(16):
        piece = (result_ref[c] + product[c]) * gain_ref[c // 8, c % 8 : c % 8 + 1, :64]
        result_ref[c] = piece
        power = power + piece * piece
    power = jnp.sum(power, axis=0, keepdims=True)
    part_ref[...] = jnp.concatenate([power, power], axis=1)

    def total(n):
        return remote(
            part_ref,
            plane_ref.at[pl.ds(n, 1)],
            plane_send.at[n],
            plane_recv.at[n],
            at(n // RING, n % RING, core),
        )

    for n in FAR_FIRST:
        total(n).start()
    plane_ref[0:1, :] = part_ref[...]
    other = remote(
        result_ref.at[pl.ds((1 - core) * 8, 8)],
        other_ref,
        other_sem.at[0],
        other_sem.at[1],
        partner,
    )
    other.start()

    for copy in [*ones, *rx, *crossings]:
        copy.wait_send()

    def left(slot, carry):
        for link in range(OWN):
            flow(link, 0, slot, True).wait_send()
        return carry

    lax.fori_loop(0, SLOTS, left, 0)
    other.wait()

    def arrived(n, carry):
        total(n).wait()
        return carry

    lax.fori_loop(1, RING * RING, arrived, 0)
    sum_ref[...] = jnp.sum(plane_ref[...], axis=0, keepdims=True)
    mate = remote(sum_ref, mate_ref, mate_sem.at[0], mate_sem.at[1], partner)
    mate.start()

    def scale(ref):
        return lax.rsqrt(ref[:, :64] / 32768.0 + 1e-05)

    out_ref[core] = result_ref[pl.ds(core * 8, 8)] * scale(sum_ref)
    mate.wait()
    out_ref[1 - core] = other_ref[...] * scale(mate_ref)


def put_out(result_ref, out_ref, sem):
    copy = pltpu.make_async_copy(result_ref, out_ref, sem)
    copy.start()
    copy.wait()


def per_device(receivers, sources, coupling, lag_basis, source_order):
    lags, basis_count = lag_basis.shape
    bf16, f32 = jnp.bfloat16, jnp.float32
    dma = pltpu.SemaphoreType.DMA
    anywhere = pl.BlockSpec(memory_space=pl.ANY)
    result = pl.pallas_call(
        kernel,
        out_shape=pltpu.VMEM((2, 8, 32, 64), f32),
        in_specs=[anywhere] * 7,
        out_specs=pl.BlockSpec(memory_space=pltpu.VMEM),
        scratch_shapes=[
            pltpu.SMEM(coupling.shape, f32),
            pltpu.SMEM(source_order.shape, jnp.int32),
            pltpu.SMEM((RING * RING * 3 * OWN,), jnp.int32),
            pltpu.VMEM((basis_count, lags), f32),
            pltpu.VMEM((lags, 512), f32),
            pltpu.VMEM((ROWS, 2, 2, 8, 512), bf16),
            pltpu.VMEM((2, 8, 128), f32),
            pltpu.VMEM((2, OWN, *PIECE), bf16),
            pltpu.VMEM((2, 2, *PIECE), bf16),
            pltpu.VMEM((2, CHUNKS, 32, 128), bf16),
            pltpu.VMEM((CHUNKS, 32, 128), bf16),
            pltpu.VMEM((OWN * SLOTS, 32, 128), bf16),
            pltpu.VMEM((CHUNKS, 512, 512), bf16),
            pltpu.VMEM((16, 32, 64), f32),
            pltpu.VMEM((8, 32, 64), f32),
            pltpu.VMEM((1, 128), f32),
            pltpu.VMEM((RING * RING, 128), f32),
            pltpu.VMEM((1, 128), f32),
            pltpu.VMEM((1, 128), f32),
            dma((6,)),
            dma((2 * ROWS,)),
            dma((2 * ROWS,)),
            dma((2,)),
            dma((2 * OWN,)),
            dma((2 * OWN,)),
            dma((4 * ROWS,)),
            dma((4 * ROWS,)),
            dma((OWN * SLOTS,)),
            dma((OWN * SLOTS,)),
            dma((2,)),
            dma((RING * RING,)),
            dma((RING * RING,)),
            dma((2,)),
            *[pltpu.VMEM((OWN * HOPS, 32, 128), bf16)] * LAG,
            *[pltpu.VMEM((OWN, 32, 128), bf16)] * (CHUNKS - LAG),
        ],
        compiler_params=pltpu.CompilerParams(collective_id=0, has_side_effects=True),
    )(
        receivers,
        sources.reshape(2, ROWS, 2, 32, 512),
        lag_basis.T,
        jnp.asarray(phase_table(256, lags)),
        coupling,
        source_order,
        jnp.asarray(tree_tables()),
    )
    return pl.pallas_call(
        put_out,
        out_shape=jax.ShapeDtypeStruct(result.shape, f32),
        in_specs=[pl.BlockSpec(memory_space=pltpu.VMEM)],
        out_specs=anywhere,
        scratch_shapes=[dma],
        compiler_params=pltpu.CompilerParams(vmem_limit_bytes=1 << 20),
    )(result)


def solution(mesh):
    return jax.shard_map(
        per_device,
        mesh=mesh,
        in_specs=(P("win", "chan", None), P("win", "chan", None), P("chan"), P(), P()),
        out_specs=P(None, "chan", None, "win"),
        check_vma=False,
    )
```

```python
import functools
import math

import jax
import jax.numpy as jnp
import numpy as np
from jax import lax
from jax.experimental import pallas as pl
from jax.experimental.pallas import tpu as pltpu
from jax.sharding import PartitionSpec as P

MESH = pl.DeviceIdType.MESH
RING = 8
ROWS = 4
TURNS = ((1, 0), (0, 1), (-1, 0), (0, -1))
LINKS = TURNS + tuple((2 * y, 2 * z) for y, z in TURNS)
TREES = (
    (
        (2, 6, 2, 2, 2, 2, 2, 2),
        (-1, 1, 5, 5, 5, 7, 7, 3),
        (0, 1, 4, 2, 2, 2, 0, 7),
        (4, 3, 5, 4, 5, 4, 4, 5),
        (0, 3, 0, 0, 0, 0, 0, 2),
        (4, 5, 4, 4, 4, 4, 4, 3),
        (0, 2, 0, 2, 2, 6, 0, 2),
        (3, 6, 7, 6, 6, 5, 5, 6),
    ),
    (
        (6, 1, 6, 6, 6, 6, 7, 6),
        (2, 3, 2, 2, 1, 6, 6, 6),
        (-1, 3, 5, 1, 5, 7, 3, 3),
        (0, 2, 0, 0, 7, 0, 2, 0),
        (4, 1, 4, 5, 7, 3, 7, 5),
        (0, 0, 1, 0, 0, 0, 0, 4),
        (4, 0, 4, 4, 4, 4, 4, 0),
        (6, 3, 6, 1, 5, 2, 4, 4),
    ),
)
HOPS = 4
CHUNKS = 2 * ROWS
LAG = 6
SLOTS = CHUNKS + (HOPS - 1) * LAG
OWN = len(LINKS)
LONG_FIRST = (4, 5, 6, 7, 0, 1, 2, 3)
FAR_FIRST = sorted(
    range(1, RING * RING),
    key=lambda n: -sum(min(d, RING - d) for d in divmod(n, RING)),
)
PIECE = (ROWS, 32, 128)
WINDOWS = ((0, 0), (0, 1), (1, 0), (3, 0), (2, 0), (1, 1), (3, 1), (2, 1))


def turn(node, times):
    for _ in range(times % 4):
        node = ((-node[1]) % RING, node[0])
    return node


def step_from(node, link, sign=1):
    return tuple((node[i] + sign * LINKS[link][i]) % RING for i in range(2))


def tree_tables():
    def reached(tree, node):
        y, z = turn(node, -tree)
        link = TREES[tree // 4][y][z]
        return -1 if link < 0 else link // 4 * 4 + (link + tree) % 4

    def depth(tree, node):
        count = 0
        while (link := reached(tree, node)) >= 0:
            node = step_from(node, link, -1)
            count += 1
        return count

    table = np.zeros((RING * RING, 3 * OWN), np.int32)
    for y in range(RING):
        for z in range(RING):
            row = table[y * RING + z]
            for tree in range(OWN):
                link, level = reached(tree, (y, z)), depth(tree, (y, z))
                assert level <= HOPS
                row[OWN + tree] = 0 if level == 0 else link * HOPS + level - 1
                row[2 * OWN + tree] = level
                for out in range(OWN):
                    if reached(tree, step_from((y, z), out)) == out:
                        row[out] = OWN if level == 0 else link
    return table.reshape(-1)


def phase_table(band, lags):
    turns = np.arange(lags)[:, None] - lags // 2
    phase = (turns * np.arange(band)[None, :]) % (2 * band) * (math.pi / band)
    return np.concatenate([np.cos(phase), np.sin(phase)], axis=1).astype(np.float32)


def kernel(
    receivers_ref,
    sources_ref,
    basis_hbm,
    phase_hbm,
    coupling_hbm,
    order_hbm,
    table_hbm,
    out_ref,
    coupling_ref,
    order_ref,
    table_ref,
    basis_ref,
    phase_ref,
    rx_ref,
    gain_ref,
    taken_ref,
    pick_ref,
    both_ref,
    own_ref,
    send_ref,
    rows_ref,
    result_ref,
    other_ref,
    part_ref,
    plane_ref,
    sum_ref,
    mate_ref,
    local_sem,
    rx_send,
    rx_recv,
    gain_sem,
    one_send,
    one_recv,
    x_send,
    x_recv,
    flow_send,
    flow_recv,
    other_sem,
    plane_send,
    plane_recv,
    mate_sem,
    *came_refs,
):
    chan, me_x = lax.axis_index("chan"), lax.axis_index("win")
    core = chan % 2
    me_y = chan // 2 % RING
    me_z = chan // (2 * RING)

    def at(dy, dz, which, dx=0):
        y, z = (me_y + dy) % RING, (me_z + dz) % RING
        return ((z * RING + y) * 2 + which, (me_x + dx) % ROWS)

    def remote(src, dst, send, recv, device):
        return pltpu.make_async_remote_copy(
            src_ref=src, dst_ref=dst, send_sem=send, recv_sem=recv, device_id=device, device_id_type=MESH
        )

    partner = at(0, 0, 1 - core)
    x_mates = [at(0, 0, which, d) for which in (core, 1 - core) for d in range(1, ROWS)]
    links = [at(dy, dz, core) for dy, dz in LINKS]

    loads = [
        pltpu.make_async_copy(basis_hbm, basis_ref, local_sem.at[0]),
        pltpu.make_async_copy(phase_hbm, phase_ref, local_sem.at[1]),
        pltpu.make_async_copy(receivers_ref, rx_ref.at[0, core], local_sem.at[2]),
        pltpu.make_async_copy(coupling_hbm, coupling_ref, local_sem.at[3]),
        pltpu.make_async_copy(order_hbm, order_ref, local_sem.at[4]),
        pltpu.make_async_copy(table_hbm, table_ref, local_sem.at[5]),
    ]
    barrier = pltpu.get_barrier_semaphore()
    greeted = [partner, *links, *x_mates]
    for device in greeted:
        pl.semaphore_signal(barrier, inc=1, device_id=device, device_id_type=MESH)
    for load in loads:
        load.start()
    pl.semaphore_wait(barrier, len(greeted))

    ones = [
        remote(
            sources_ref.at[half, :, tree // 4, :, pl.ds(128 * (tree % 4), 128)],
            taken_ref.at[half, tree],
            one_send.at[half * OWN + tree],
            one_recv.at[half * OWN + tree],
            links[tree],
        )
        for half in range(2)
        for tree in range(OWN)
    ]
    for half in range(2):
        for tree in LONG_FIRST:
            ones[half * OWN + tree].start()
    rx = []
    for n, (dx, flip) in enumerate((dx, flip) for flip in (0, 1) for dx in range(ROWS)):
        if n:
            rx.append(
                remote(
                    receivers_ref,
                    rx_ref.at[(ROWS - dx) % ROWS, core],
                    rx_send.at[n],
                    rx_recv.at[n],
                    at(0, 0, core if flip == 0 else 1 - core, dx),
                )
            )
    for copy in rx:
        copy.start()
    loads[3].wait()
    for c in range(8):
        gain_ref[core, c : c + 1, :] = jnp.full((1, 128), coupling_ref[c], jnp.float32)
    gains = remote(gain_ref.at[core], gain_ref.at[core], gain_sem.at[0], gain_sem.at[1], partner)
    gains.start()

    loads[0].wait()
    loads[1].wait()
    tables = lax.dot_general(
        basis_ref[...],
        phase_ref[...],
        (((1,), (0,)), ((), ())),
        precision=lax.Precision.HIGHEST,
        preferred_element_type=jnp.float32,
    )
    band = tables.shape[1] // 2
    cosine, sine = tables[:, :band], tables[:, band:]

    loads[2].wait()
    for copy in rx:
        copy.wait_recv()

    def project(n, carry):
        slab, half, which = n // 4, n // 2 % 2, n % 2
        place = jnp.where(slab == 1, 2, jnp.where(slab == 2, 4, 3)) + 3 * half
        place = jnp.where(slab == 0, half, place)
        spectra = rx_ref[slab, which, half].astype(jnp.float32)
        for c in range(8):
            real, imag = spectra[c : c + 1, :band], spectra[c : c + 1, band:]
            both = jnp.concatenate([real * cosine - imag * sine, real * sine + imag * cosine], axis=1)
            first = pl.multiple_of(which * 256 + c * 32, 32)
            rows_ref[place, pl.ds(first, 32), :] = both.astype(jnp.bfloat16)
        return carry

    lax.fori_loop(0, 2 * CHUNKS, project, 0)

    loads[4].wait()
    loads[5].wait()
    owners = [order_ref[b] for b in range(2)]
    roots = [(o // 2 % RING, o // (2 * RING), o % 2) for o in owners]
    relative = [((me_y - y + RING) % RING, (me_z - z + RING) % RING) for y, z, _ in roots]

    crossings = []
    for half in range(2):
        for tree in range(OWN):
            ones[half * OWN + tree].wait_recv()
        for b in range(2):
            kept = taken_ref[half, 0]
            for tree in range(1, OWN):
                dy, dz = LINKS[tree]
                here = jnp.logical_and(relative[b][0] == dy % RING, relative[b][1] == dz % RING)
                kept = jnp.where(here, taken_ref[half, tree], kept)
            pick_ref[half, b] = kept
        for n in range(1, 2 * ROWS):
            flip, dx = divmod(n, ROWS)
            which = core if flip == 0 else 1 - core
            place = WINDOWS.index(((ROWS - dx) % ROWS, half))
            crossings.append(
                remote(
                    pick_ref.at[half, which, (me_x + dx) % ROWS],
                    both_ref.at[core, place],
                    x_send.at[half * 2 * ROWS + n],
                    x_recv.at[half * 2 * ROWS + n],
                    at(0, 0, which, dx),
                )
            )
        for n in (2, ROWS + 2, 1, 3, ROWS + 1, ROWS + 3, ROWS):
            crossings[half * (2 * ROWS - 1) + n - 1].start()
        both_ref[core, half] = pick_ref[half, core, me_x]
    mine = core == 0
    root_core = jnp.where(mine, roots[0][2], roots[1][2])

    rel_y = jnp.where(mine, relative[0][0], relative[1][0])
    rel_z = jnp.where(mine, relative[0][1], relative[1][1])
    entry = (rel_y * RING + rel_z) * 3 * OWN
    forward = [table_ref[entry + link] for link in range(OWN)]
    place_of = [table_ref[entry + OWN + tree] for tree in range(OWN)]
    level_of = [table_ref[entry + 2 * OWN + tree] for tree in range(OWN)]

    def landing(link, hop, lane):
        if isinstance(hop, int) and hop == HOPS:
            return came_refs[LAG + lane].at[link]
        return came_refs[lane].at[link * HOPS + hop]

    def flow(link, hop, lane, leaving=False):
        number = link * SLOTS + hop * LAG + lane
        return remote(
            send_ref.at[number],
            came_refs[0].at[0] if leaving else landing(link, hop, lane),
            flow_send.at[number],
            flow_recv.at[number],
            links[link],
        )

    def pass_on(hop, lane, own):
        heard = []
        if not (isinstance(hop, int) and hop == 0):
            for link in range(OWN):
                flow(link, hop - 1, lane).wait_recv()
            heard = [came_refs[lane][link * HOPS + hop - 1] for link in range(OWN)]
        for link in LONG_FIRST:
            value = heard[0] if own is None else own
            for n, got in enumerate(heard):
                value = jnp.where(forward[link] == n, got, value)
            send_ref[link * SLOTS + hop * LAG + lane] = value
            flow(link, hop, lane).start()

    for slot in range(CHUNKS):
        slab, half = WINDOWS[slot]
        dx = (ROWS - slab) % ROWS
        for n in (dx, ROWS + dx):
            if n:
                crossings[half * (2 * ROWS - 1) + n - 1].wait_recv()
        own = jnp.where(root_core == 0, both_ref[0, slot], both_ref[1, slot])
        own_ref[slot] = own
        pass_on(slot // LAG, slot % LAG, own)
    for lane in range(CHUNKS - LAG, LAG):
        pass_on(1, lane, None)

    def later(hop, carry):
        for lane in range(LAG):
            pass_on(hop, lane, None)
        return carry

    lax.fori_loop(2, HOPS, later, 0)
    for lane in range(CHUNKS - LAG):
        pass_on(HOPS, lane, None)

    for chunk in range(CHUNKS):
        late, lane = divmod(chunk, LAG)
        for link in range(OWN):
            if late:
                flow(link, HOPS, lane).wait_recv()
            elif lane >= CHUNKS - LAG:
                flow(link, HOPS - 1, lane).wait_recv()
        halves = []
        for half in range(2):
            pieces = []
            for tree in range(4 * half, 4 * half + 4):
                if late:
                    last = level_of[tree] == HOPS
                    got = came_refs[lane][place_of[tree] + jnp.where(last, 0, 1)]
                    got = jnp.where(last, came_refs[LAG + lane][place_of[tree] // HOPS], got)
                else:
                    got = came_refs[lane][place_of[tree]]
                pieces.append(jnp.where(level_of[tree] == 0, own_ref[chunk], got))
            halves.append(jnp.concatenate(pieces, axis=1))
        product = lax.dot_general(
            rows_ref[chunk],
            jnp.concatenate(halves, axis=0),
            (((1,), (1,)), ((), ())),
            preferred_element_type=jnp.float32,
        )
        product = product.reshape(16, 32, 64)
        if chunk == 0:
            result_ref[...] = product
        elif chunk < CHUNKS - 1:
            result_ref[...] += product
    gains.wait()
    power = jnp.zeros((32, 64), jnp.float32)
    for c in range(16):
        piece = (result_ref[c] + product[c]) * gain_ref[c // 8, c % 8 : c % 8 + 1, :64]
        result_ref[c] = piece
        power = power + piece * piece
    power = jnp.sum(power, axis=0, keepdims=True)
    part_ref[...] = jnp.concatenate([power, power], axis=1)

    def total(n):
        return remote(
            part_ref,
            plane_ref.at[pl.ds(n, 1)],
            plane_send.at[n],
            plane_recv.at[n],
            at(n // RING, n % RING, core),
        )

    for n in FAR_FIRST:
        total(n).start()
    plane_ref[0:1, :] = part_ref[...]
    other = remote(
        result_ref.at[pl.ds((1 - core) * 8, 8)],
        other_ref,
        other_sem.at[0],
        other_sem.at[1],
        partner,
    )
    other.start()

    for copy in [*ones, *rx, *crossings]:
        copy.wait_send()

    def left(slot, carry):
        for link in range(OWN):
            flow(link, 0, slot, True).wait_send()
        return carry

    lax.fori_loop(0, SLOTS, left, 0)
    other.wait()

    def arrived(n, carry):
        total(n).wait()
        return carry

    lax.fori_loop(1, RING * RING, arrived, 0)
    sum_ref[...] = jnp.sum(plane_ref[...], axis=0, keepdims=True)
    mate = remote(sum_ref, mate_ref, mate_sem.at[0], mate_sem.at[1], partner)
    mate.start()

    def scale(ref):
        return lax.rsqrt(ref[:, :64] / 32768.0 + 1e-05)

    out_ref[core] = result_ref[pl.ds(core * 8, 8)] * scale(sum_ref)
    mate.wait()
    out_ref[1 - core] = other_ref[...] * scale(mate_ref)


def put_out(result_ref, out_ref, sem):
    copies = [
        pltpu.make_async_copy(result_ref.at[n // 2, pl.ds(n % 2 * 4, 4)], out_ref.at[n // 2, pl.ds(n % 2 * 4, 4)], sem.at[n])
        for n in range(4)
    ]
    for copy in copies:
        copy.start()
    for copy in copies:
        copy.wait()


def per_device(receivers, sources, coupling, lag_basis, source_order):
    lags, basis_count = lag_basis.shape
    bf16, f32 = jnp.bfloat16, jnp.float32
    dma = pltpu.SemaphoreType.DMA
    anywhere = pl.BlockSpec(memory_space=pl.ANY)
    result = pl.pallas_call(
        kernel,
        out_shape=pltpu.VMEM((2, 8, 32, 64), f32),
        in_specs=[anywhere] * 7,
        out_specs=pl.BlockSpec(memory_space=pltpu.VMEM),
        scratch_shapes=[
            pltpu.SMEM(coupling.shape, f32),
            pltpu.SMEM(source_order.shape, jnp.int32),
            pltpu.SMEM((RING * RING * 3 * OWN,), jnp.int32),
            pltpu.VMEM((basis_count, lags), f32),
            pltpu.VMEM((lags, 512), f32),
            pltpu.VMEM((ROWS, 2, 2, 8, 512), bf16),
            pltpu.VMEM((2, 8, 128), f32),
            pltpu.VMEM((2, OWN, *PIECE), bf16),
            pltpu.VMEM((2, 2, *PIECE), bf16),
            pltpu.VMEM((2, CHUNKS, 32, 128), bf16),
            pltpu.VMEM((CHUNKS, 32, 128), bf16),
            pltpu.VMEM((OWN * SLOTS, 32, 128), bf16),
            pltpu.VMEM((CHUNKS, 512, 512), bf16),
            pltpu.VMEM((16, 32, 64), f32),
            pltpu.VMEM((8, 32, 64), f32),
            pltpu.VMEM((1, 128), f32),
            pltpu.VMEM((RING * RING, 128), f32),
            pltpu.VMEM((1, 128), f32),
            pltpu.VMEM((1, 128), f32),
            dma((6,)),
            dma((2 * ROWS,)),
            dma((2 * ROWS,)),
            dma((2,)),
            dma((2 * OWN,)),
            dma((2 * OWN,)),
            dma((4 * ROWS,)),
            dma((4 * ROWS,)),
            dma((OWN * SLOTS,)),
            dma((OWN * SLOTS,)),
            dma((2,)),
            dma((RING * RING,)),
            dma((RING * RING,)),
            dma((2,)),
            *[pltpu.VMEM((OWN * HOPS, 32, 128), bf16)] * LAG,
            *[pltpu.VMEM((OWN, 32, 128), bf16)] * (CHUNKS - LAG),
        ],
        compiler_params=pltpu.CompilerParams(collective_id=0, has_side_effects=True),
    )(
        receivers,
        sources.reshape(2, ROWS, 2, 32, 512),
        lag_basis.T,
        jnp.asarray(phase_table(256, lags)),
        coupling,
        source_order,
        jnp.asarray(tree_tables()),
    )
    return pl.pallas_call(
        put_out,
        out_shape=jax.ShapeDtypeStruct(result.shape, f32),
        in_specs=[pl.BlockSpec(memory_space=pltpu.VMEM)],
        out_specs=anywhere,
        scratch_shapes=[dma((4,))],
        compiler_params=pltpu.CompilerParams(vmem_limit_bytes=1 << 20),
    )(result)


def solution(mesh):
    return jax.shard_map(
        per_device,
        mesh=mesh,
        in_specs=(P("win", "chan", None), P("win", "chan", None), P("chan"), P(), P()),
        out_specs=P(None, "chan", None, "win"),
        check_vma=False,
    )
```
